512 devices in a mesh: case: 8 (over z_hi, y), tile: 64 (over z_lo, x, core).
Axes of the slice: x: 4, y: 4, z: 16 (z_hi: 2, z_lo: 8; z = z_hi * 8 + z_lo), core: 2. Of those that a mesh axis runs over, the one named last changes fastest.
Arguments:
- density: float32 [512, 64, 256], P('tile', 'case'), may hold values from 0.05 to 1
- heat_power: float32 [8, 512, 64, 256], P('case', 'tile'), may hold values from 0.2 to 15, as said below
- laser_mask: int32 [8, 512, 64, 256], P('case', 'tile'), may hold values 0 or 1
- sink_mask: int32 [512, 64, 256], P('tile'), may hold values 0 or 1
Outputs:
- sensitivity: float32 [512, 64, 256], P('tile', 'case')
- objective: float32 [8], P('case')
The draws below stay inside these ranges and needn't reach their ends.
Inputs may be any that keep to these rules, and one draw needn't show every extreme that they name: `heat_power`: positive heat power of each voxel and case.
All inputs are finite; a program needn't handle non-finite values. Where the reference program divides by a largest or mean magnitude, that divisor is 1e-20 or more. No bound on the sum of `laser_mask` or of `sink_mask` on one device may be relied on, other than what follows from the above.
Results may differ from the reference program's by a relative error of at most 0.0001.
Values sent between devices are 32-bit elements; how exact they have to be, the bound alone decides.
A program may use at most 64 MiB of HBM per device.

```python
import math
import jax
import jax.numpy as jnp
from jax import lax

NZ = 256
SWEEPS = 6
NX = 512
NY = 64
CASES = 8


def draw_heat_power(key, part):
    base_key = jax.random.fold_in(key, 11)
    full_shape = (CASES, NX, NY, NZ)
    position = jnp.arange(NX, dtype=jnp.float32) / max(NX - 1, 1)
    ramp_up = position.reshape(1, NX, 1, 1)
    log_low = math.log(0.2)
    log_high = math.log(5.0)
    base_draw = jnp.exp(jax.random.uniform(base_key, full_shape, jnp.float32, log_low, log_high))
    return base_draw * (1.0 + 2.0 * ramp_up)


def with_ends(array, key, low, top_value):
    shape = array.shape
    spot = [jax.random.randint(jax.random.fold_in(key, axis), (), 0, shape[axis]) for axis in range(len(shape))]
    array = array.at[tuple(spot)].set(low)
    longest = shape.index(max(shape))
    spot[longest] = (spot[longest] + 1) % shape[longest]
    return array.at[tuple(spot)].set(top_value)


def levels(key, shape, shards, smallest, largest):
    level = 1.0
    for dim, parts in shards:
        steps = jax.random.uniform(jax.random.fold_in(jax.random.fold_in(key, 6), dim), (parts,), jnp.float32, smallest / len(shards), largest / len(shards))
        level = level * jnp.repeat(jnp.exp(steps), shape[dim] // parts).reshape((-1,) + (1,) * (len(shape) - 1 - dim))
    return level


def setup_inputs(seed: int = 0) -> dict:
    key_list = jax.random.split(jax.random.key(seed), 5)
    return {
        "density": jnp.clip(0.05 + 0.95 * jax.random.uniform(key_list[0], (NX, NY, NZ), jnp.float32) ** levels(key_list[0], (NX, NY, NZ), ((0, 64), (1, 8)), -0.2, 0.2), 0.05, 1.0),
        "heat_power": draw_heat_power(jax.random.fold_in(key_list[4], 71), 0),
        "laser_mask": with_ends((jax.random.randint(key_list[2], (CASES, NX, NY, NZ), 0, 4) < 1).astype(jnp.int32), jax.random.fold_in(key_list[2], 1), 0, 1),
        "sink_mask": with_ends((jax.random.randint(key_list[3], (NX, NY, NZ), 0, 16) < 1).astype(jnp.int32), jax.random.fold_in(key_list[3], 1), 0, 1),
    }


heat_loss = 0.02
low_cond = 0.01
eig_low = 0.08
eig_high = 2.0


def pad_axis(field, along, leading, trailing):
    along = along % field.ndim
    widths = [(0, 0)] * field.ndim
    widths[along] = (leading, trailing)
    return jnp.pad(field, widths)


def lower_part(field, along):
    along = along % field.ndim
    return lax.slice_in_dim(field, 0, field.shape[along] - 1, axis=along)


def upper_part(field, along):
    along = along % field.ndim
    return lax.slice_in_dim(field, 1, field.shape[along], axis=along)


def flux_sum(field, face_cond, along):
    heat_flow = face_cond * (lower_part(field, along) - upper_part(field, along))
    return pad_axis(heat_flow, along, 0, 1) - pad_axis(heat_flow, along, 1, 0)


def interface_heatflow_pairs(left_field, right_field, along):
    multiplied_pieces = (lower_part(left_field, along) - upper_part(left_field, along)) * (lower_part(right_field, along) - upper_part(right_field, along))
    return pad_axis(multiplied_pieces, along, 0, 1) + pad_axis(multiplied_pieces, along, 1, 0)


def beside_sum(field, along):
    return pad_axis(upper_part(field, along), along, 0, 1) + pad_axis(lower_part(field, along), along, 1, 0)


def edge_count(position, extent):
    return (position > 0).astype(jnp.float32) + (position < extent - 1).astype(jnp.float32)


def polynomial_relaxer(right_side, operate, diagonal_entries, unfixed_cells):
    centre = 0.5 * (eig_high + eig_low)
    half_width = 0.5 * (eig_high - eig_low)
    spread_ratio = centre / half_width
    weight_prev = 1.0 / spread_ratio
    iterate = (unfixed_cells * right_side / diagonal_entries) / centre
    update = iterate
    for sweep_idx in range(1, SWEEPS):
        weight_next = 1.0 / (2.0 * spread_ratio - weight_prev)
        residual_part = right_side - operate(iterate)
        update = (weight_next * weight_prev) * update + (2.0 * weight_next / half_width) * (unfixed_cells * residual_part / diagonal_entries)
        iterate = iterate + update
        weight_prev = weight_next
    return iterate


def reference(density, heat_power, laser_mask, sink_mask):
    grid_x, grid_y, grid_z = density.shape
    counts = 2.0 + edge_count(jnp.arange(grid_x), grid_x)[:, None, None] + edge_count(jnp.arange(grid_y), grid_y)[None, :, None] + edge_count(jnp.arange(grid_z), grid_z)[None, None, :]
    beside_all = beside_sum(density, 0) + beside_sum(density, 1) + beside_sum(density, 2)
    physical = (2.0 * density + beside_all) / counts
    conduct = low_cond + (1.0 - low_cond) * (physical * physical * physical)
    face_rows = 0.5 * (lower_part(conduct, 0) + upper_part(conduct, 0))
    face_cols = 0.5 * (lower_part(conduct, 1) + upper_part(conduct, 1))
    face_deep = 0.5 * (lower_part(conduct, 2) + upper_part(conduct, 2))
    diagonal_entries = heat_loss + pad_axis(face_rows, 0, 0, 1) + pad_axis(face_rows, 0, 1, 0)
    diagonal_entries = diagonal_entries + pad_axis(face_cols, 1, 0, 1) + pad_axis(face_cols, 1, 1, 0)
    diagonal_entries = diagonal_entries + pad_axis(face_deep, 2, 0, 1) + pad_axis(face_deep, 2, 1, 0)
    unfixed_cells = 1.0 - sink_mask.astype(jnp.float32)

    def operate(field):
        return heat_loss * field + flux_sum(field, face_rows, -3) + flux_sum(field, face_cols, -2) + flux_sum(field, face_deep, -1)

    def one_case(accumulated_amount, inputs):
        source_power, lasers = inputs
        desired_values = lasers.astype(jnp.float32)
        source_term = desired_values * source_power
        converged_state = polynomial_relaxer(jnp.stack([source_term, desired_values]), operate, diagonal_entries, unfixed_cells)
        thermal_state_grid = converged_state[0]
        dual_state_values = converged_state[1]
        multiplied_pieces = interface_heatflow_pairs(thermal_state_grid, dual_state_values, 0) + interface_heatflow_pairs(thermal_state_grid, dual_state_values, 1) + interface_heatflow_pairs(thermal_state_grid, dual_state_values, 2)
        return accumulated_amount + multiplied_pieces, jnp.sum(desired_values * thermal_state_grid)

    accumulated_amount, objective = lax.scan(one_case, jnp.zeros(density.shape, jnp.float32), (heat_power, laser_mask))
    sens_phys = (-1.5 * (1.0 - low_cond)) * (physical * physical) * accumulated_amount
    weighted = sens_phys / counts
    sens_density = 2.0 * weighted + beside_sum(weighted, 0) + beside_sum(weighted, 1) + beside_sum(weighted, 2)
    magnitude = jnp.mean(jnp.abs(sens_density))
    return sens_density / (magnitude + 1e-6), objective
```

```python
import functools

import jax
import jax.numpy as jnp
from jax import lax
from jax.experimental import pallas as pl
from jax.experimental.pallas import tpu as pltpu
from jax.sharding import PartitionSpec as P

SWEEPS = 6
heat_loss = 0.02
low_cond = 0.01
eig_low = 0.08
eig_high = 2.0

MESH = pl.DeviceIdType.MESH
YD = 4
ZH = 2
XC = 8
R = 8
EXT = 3 * R


def horner_coefficients():
    centre = 0.5 * (eig_high + eig_low)
    half = 0.5 * (eig_high - eig_low)
    ratio = centre / half
    weight = 1.0 / ratio
    x = [1.0 / centre] + [0.0] * (SWEEPS - 1)
    s = list(x)
    for _ in range(1, SWEEPS):
        nxt = 1.0 / (2.0 * ratio - weight)
        r = [-a for a in x]
        r[0] += 1.0
        for k in range(1, SWEEPS):
            r[k] += x[k - 1]
        s = [nxt * weight * a + 2.0 * nxt / half * b for a, b in zip(s, r)]
        x = [a + b for a, b in zip(x, s)]
        weight = nxt
    return x


COEF = horner_coefficients()
LEAD = COEF[-1]


def kernel(
    tiles,
    dens_in, heat_in, laser_in, sink_in,
    sens_out, obj_out,
    dens, heat, laser, sink, src, cond, wgt, kxm, kxp, kym, kyp, kzm, kzp, bias, ya, yb,
    part, rfar, rnear, fsum, rz, qsum, qhalo, sens, msg, arx, ary, arz,
    lsem, s_y, r_y, s_z, r_z, s_yf, r_yf, s_t, r_t, s_h, r_h, s_p, r_p, s_pz, r_pz, s_q, r_q,
    s_ax, r_ax, s_ay, r_ay, s_az, r_az,
):
    zl_n = tiles // XC
    z_n = ZH * zl_n
    c = lax.axis_index("case")
    t = lax.axis_index("tile")
    zh = c // YD
    yy = c % YD
    zl = t // XC
    xc = t % XC
    z = zh * zl_n + zl
    has_left = t > 0
    has_right = t < tiles - 1
    halves = dens.shape[1]
    width = 128 * halves

    def y_case(d):
        return zh * YD + (yy + d) % YD

    def z_dev(d):
        zz = (z + d) % z_n
        return {"case": (zz // zl_n) * YD + yy, "tile": (zz % zl_n) * XC + xc}

    def x_tile(d):
        return zl * XC + (xc + d) % XC

    barrier = pltpu.get_barrier_semaphore()

    def greet(dev):
        pl.semaphore_signal(barrier, inc=1, device_id=dev, device_id_type=MESH)

    for d in range(1, z_n):
        greet(z_dev(d))
    for d in range(1, YD):
        greet({"case": y_case(d), "tile": t})
    for d in range(1, XC):
        greet({"case": c, "tile": x_tile(d)})

    @pl.when(has_left)
    def _():
        greet({"case": c, "tile": t - 1})

    @pl.when(has_right)
    def _():
        greet({"case": c, "tile": t + 1})

    slab = pl.ds(pl.multiple_of(c * R, R), R)
    loads = []
    for h in range(halves):
        lanes = pl.ds(h * 128, 128)
        loads.append([
            pltpu.make_async_copy(dens_in.at[:, :, lanes], dens.at[pl.ds(R, R), h, slab, :], lsem.at[h, 0]),
            pltpu.make_async_copy(heat_in.at[0, :, :, lanes], heat.at[:, h], lsem.at[h, 1]),
            pltpu.make_async_copy(laser_in.at[0, :, :, lanes], laser.at[:, h], lsem.at[h, 2]),
            pltpu.make_async_copy(sink_in.at[:, :, lanes], sink.at[pl.ds(R, R), h], lsem.at[h, 3]),
        ])
    for k in range(4):
        for h in range(halves):
            loads[h][k].start()

    @pl.when(t == 0)
    def _():
        dens[0:R] = jnp.zeros((R,) + dens.shape[1:], jnp.float32)
        src[2:R] = jnp.zeros((R - 2,) + src.shape[1:], jnp.float32)
        sink[2:R] = jnp.zeros((R - 2,) + sink.shape[1:], jnp.int32)
        qhalo[0] = jnp.zeros(qhalo.shape[1:], jnp.float32)

    @pl.when(t == tiles - 1)
    def _():
        dens[2 * R:] = jnp.zeros((R,) + dens.shape[1:], jnp.float32)
        src[2 * R:3 * R - 2] = jnp.zeros((R - 2,) + src.shape[1:], jnp.float32)
        sink[2 * R:3 * R - 2] = jnp.zeros((R - 2,) + sink.shape[1:], jnp.int32)
        qhalo[1] = jnp.zeros(qhalo.shape[1:], jnp.float32)

    for k in range(3):
        for h in range(halves):
            loads[h][k].wait()

    def row_load(ref, l, j):
        return jnp.concatenate([ref[l, h, pl.ds(j, R, stride=R), :] for h in range(halves)], axis=1)

    def make_source(l, carry):
        for j in range(R):
            src[l + R, j] = row_load(heat, l, j) * row_load(laser, l, j).astype(jnp.float32)
        return carry

    lax.fori_loop(0, R, make_source, 0)

    for h in range(halves):
        loads[h][3].wait()
    pl.semaphore_wait(
        barrier, (z_n - 1) + (YD - 1) + (XC - 1) + has_left.astype(jnp.int32) + has_right.astype(jnp.int32)
    )

    def remote(a, b, ssem, rsem, dev):
        return pltpu.make_async_remote_copy(
            src_ref=a, dst_ref=b, send_sem=ssem, recv_sem=rsem, device_id=dev, device_id_type=MESH
        )

    def to_left(a, b, ssem, rsem):
        return remote(a, b, ssem, rsem, {"case": c, "tile": jnp.maximum(t - 1, 0)})

    def to_right(a, b, ssem, rsem):
        return remote(a, b, ssem, rsem, {"case": c, "tile": jnp.minimum(t + 1, tiles - 1)})

    own = dens.at[pl.ds(R, R), :, slab, :]
    z_copy = remote(own, own, s_z.at[0], r_z.at[0], z_dev(zl_n))
    z_copy.start()
    y_copies = []
    for d in range(1, YD):
        cp = remote(own, own, s_y.at[d - 1], r_y.at[d - 1], {"case": y_case(d), "tile": t})
        cp.start()
        y_copies.append(cp)

    halo_left = [
        to_left(src.at[pl.ds(R, R - 2)], src.at[pl.ds(2 * R, R - 2)], s_h.at[0], r_h.at[1]),
        to_left(sink.at[pl.ds(R, R - 2)], sink.at[pl.ds(2 * R, R - 2)], s_h.at[1], r_h.at[3]),
    ]
    halo_right = [
        to_right(src.at[pl.ds(R + 2, R - 2)], src.at[pl.ds(2, R - 2)], s_h.at[2], r_h.at[0]),
        to_right(sink.at[pl.ds(R + 2, R - 2)], sink.at[pl.ds(2, R - 2)], s_h.at[3], r_h.at[2]),
    ]

    def send_sides(left, right):
        @pl.when(has_left)
        def _():
            for cp in left:
                cp.start()

        @pl.when(has_right)
        def _():
            for cp in right:
                cp.start()

    send_sides(halo_left, halo_right)

    def slab_of(case):
        return pl.ds(pl.multiple_of(case * R, R), R)

    tile_copies = []

    def forward(case, order):
        here = dens.at[pl.ds(R, R), :, slab_of(case), :]
        left = to_left(here, dens.at[pl.ds(2 * R, R), :, slab_of(case), :], s_t.at[0, order], r_t.at[1, order])
        right = to_right(here, dens.at[pl.ds(0, R), :, slab_of(case), :], s_t.at[1, order], r_t.at[0, order])
        send_sides([left], [right])
        tile_copies.append((left, right))

    forward(c, 0)
    for d in range(1, YD):
        y_copies[d - 1].wait_recv()
        forward(zh * YD + (yy + YD - d) % YD, d)

    z_copy.wait_recv()
    far = (1 - zh) * YD
    far_case = far + yy
    far_ref = dens.at[pl.ds(R, R), :, slab_of(far_case), :]
    yf_copies = []
    for d in range(1, YD):
        cp = remote(far_ref, far_ref, s_yf.at[d - 1], r_yf.at[d - 1], {"case": y_case(d), "tile": t})
        cp.start()
        yf_copies.append(cp)
    forward(far_case, YD)
    for d in range(1, YD):
        yf_copies[d - 1].wait_recv()
        forward(far + (yy + YD - d) % YD, YD + d)

    @pl.when(has_left)
    def _():
        for left, right in tile_copies:
            right.wait_recv()
        for cp in halo_right:
            cp.wait_recv()

    @pl.when(has_right)
    def _():
        for left, right in tile_copies:
            left.wait_recv()
        for cp in halo_left:
            cp.wait_recv()

    lane = lax.broadcasted_iota(jnp.int32, (R, width), 1)
    sub = lax.broadcasted_iota(jnp.int32, (R, width), 0)
    z_first = lane == 0
    z_last = lane == width - 1
    y_first = sub == 0
    y_last = sub == R - 1
    zero = jnp.zeros((R, width), jnp.float32)
    one = jnp.ones((R, width), jnp.float32)
    grid_rows = tiles * R

    def z_prev(v):
        return pltpu.roll(v, 1, 1)

    def z_next(v):
        return pltpu.roll(v, width - 1, 1)

    def around(planes, j):
        before = planes[j - 1] if j > 0 else pltpu.roll(planes[R - 1], 1, 0)
        after = planes[j + 1] if j < R - 1 else pltpu.roll(planes[0], R - 1, 0)
        return before, after

    def flag(cond_):
        return cond_.astype(jnp.float32)

    def physical_step(e, carry):
        g = t * R - R + e
        nx = 2.0 + flag(g > 0) + flag(g < grid_rows - 1)
        nyz = nx + jnp.where(z_first | z_last, 1.0, 2.0)
        planes = [row_load(dens, e, j) for j in range(R)]
        for j in range(R):
            v = planes[j]
            before, after = around(planes, j)
            ny = jnp.full((R, width), 2.0)
            if j == 0:
                before = jnp.where(y_first, 0.0, before)
                ny = jnp.where(y_first, 1.0, 2.0)
            if j == R - 1:
                after = jnp.where(y_last, 0.0, after)
                ny = jnp.where(y_last, 1.0, 2.0)
            total = (
                2.0 * v + row_load(dens, e - 1, j) + row_load(dens, e + 1, j)
                + before + after
                + jnp.where(z_first, 0.0, z_prev(v)) + jnp.where(z_last, 0.0, z_next(v))
            )
            inv = 1.0 / (nyz + ny)
            phys = total * inv
            sq = phys * phys
            cond[e, j] = low_cond + (1.0 - low_cond) * (sq * phys)
            wgt[e, j] = (-1.5 * (1.0 - low_cond) * LEAD * LEAD) * sq * inv
        return carry

    lax.fori_loop(1, EXT - 1, physical_step, 0)

    def inside(g):
        return (g >= 0) & (g < grid_rows)

    def face_step(e, carry):
        g = t * R - R + e
        vm = 0.5 * flag(inside(g - 1) & inside(g))
        vp = 0.5 * flag(inside(g) & inside(g + 1))
        planes = [cond[e, j] for j in range(R)]
        for j in range(R):
            v = planes[j]
            before, after = around(planes, j)
            f_xm = vm * (cond[e - 1, j] + v)
            f_xp = vp * (cond[e + 1, j] + v)
            f_ym = 0.5 * (before + v)
            f_yp = 0.5 * (after + v)
            if j == 0:
                f_ym = jnp.where(y_first, 0.0, f_ym)
            if j == R - 1:
                f_yp = jnp.where(y_last, 0.0, f_yp)
            f_zm = jnp.where(z_first, 0.0, 0.5 * (z_prev(v) + v))
            f_zp = jnp.where(z_last, 0.0, 0.5 * (z_next(v) + v))
            diag = heat_loss + f_xm + f_xp + f_ym + f_yp + f_zm + f_zp
            free = jnp.where(row_load(sink, e, j) == 0, 1.0, 0.0)
            scale = free / diag
            kxm[e, j] = scale * f_xm
            kxp[e, j] = scale * f_xp
            kym[e, j] = scale * f_ym
            kyp[e, j] = scale * f_yp
            kzm[e, j] = scale * f_zm
            kzp[e, j] = scale * f_zp
            source = src[e, j]
            bias[0, e, j] = scale * source
            bias[1, e, j] = jnp.where(source > 0.0, scale, 0.0)
        return carry

    lax.fori_loop(2, EXT - 2, face_step, 0)

    def sweep(n, y_in, y_out):
        ratio = COEF[SWEEPS - 2 - n] / LEAD

        def step(e, carry):
            for j in range(R):
                ks = [k[e, j] for k in (kxm, kxp, kym, kyp, kzm, kzp)]
                for f in range(2):
                    v = y_in[f, e, j]
                    before = y_in[f, e, j - 1] if j > 0 else pltpu.roll(y_in[f, e, R - 1], 1, 0)
                    after = y_in[f, e, j + 1] if j < R - 1 else pltpu.roll(y_in[f, e, 0], R - 1, 0)
                    acc = ratio * bias[f, e, j]
                    acc = acc + ks[0] * y_in[f, e - 1, j]
                    acc = acc + ks[1] * y_in[f, e + 1, j]
                    acc = acc + ks[2] * before
                    acc = acc + ks[3] * after
                    acc = acc + ks[4] * z_prev(v)
                    acc = acc + ks[5] * z_next(v)
                    y_out[f, e, j] = acc
            return carry

        lax.fori_loop(3 + n, EXT - 3 - n, step, 0)

    bufs = [bias, ya, yb, ya, yb, ya]
    for n in range(SWEEPS - 1):
        sweep(n, bufs[n], bufs[n + 1])
    fin = bufs[SWEEPS - 1]

    def slab_store(row, value):
        for h in range(halves):
            part[h, pl.ds(row, R, stride=10 * R), :] = value[:, h * 128:(h + 1) * 128]

    def product_step(e, total):
        g = t * R - R + e
        l = e - R
        vm = flag(inside(g - 1))
        vp = flag(inside(g + 1))
        ps = [fin[0, e, j] for j in range(R)]
        qs = [fin[1, e, j] for j in range(R)]
        y_faces = []
        for j in range(R):
            pn = around(ps, j)[1]
            qn = around(qs, j)[1]
            face = (ps[j] - pn) * (qs[j] - qn)
            if j == R - 1:
                face = jnp.where(y_last, 0.0, face)
            y_faces.append(face)
        for j in range(R):
            p, q = ps[j], qs[j]
            acc = vm * ((p - fin[0, e - 1, j]) * (q - fin[1, e - 1, j]))
            acc = acc + vp * ((p - fin[0, e + 1, j]) * (q - fin[1, e + 1, j]))
            acc = acc + y_faces[j] + around(y_faces, j)[0]
            face = jnp.where(z_last, 0.0, (p - z_next(p)) * (q - z_next(q)))
            acc = (acc + face + z_prev(face)) * wgt[e, j]
            slab_store(l * R + j, acc)
            if j == R - 1:
                edge = jnp.where(y_first, 0.0, pltpu.roll(acc, 1, 0))
                slab_store(8 * R + l, edge)
            if j == 0:
                edge = jnp.where(y_last, 0.0, pltpu.roll(acc, R - 1, 0))
                slab_store(9 * R + l, edge)
            total = total + jnp.where(src[e, j] > 0.0, p, 0.0)
        return total

    obj_vec = lax.fori_loop(R, 2 * R, product_step, zero)

    def block(case):
        return pl.ds(pl.multiple_of(case * (10 * R), 10 * R), 10 * R)

    far_parts = []
    near_parts = []
    for d in range(1, YD):
        dest = (yy + d) % YD
        cp = remote(part.at[:, block(far + dest)], rfar.at[d - 1], s_p.at[0, d - 1], r_p.at[0, d - 1],
                    {"case": y_case(d), "tile": t})
        cp.start()
        far_parts.append(cp)
    for d in range(1, YD):
        dest = (yy + d) % YD
        cp = remote(part.at[:, block(zh * YD + dest)], rnear.at[d - 1], s_p.at[1, d - 1], r_p.at[1, d - 1],
                    {"case": y_case(d), "tile": t})
        cp.start()
        near_parts.append(cp)
    obj_part = LEAD * jnp.sum(obj_vec)
    for cp in far_parts:
        cp.wait_recv()
    base_far = far_case * (10 * R)

    def far_step(i, carry):
        rows = pl.ds(pl.multiple_of(i * R, R), R)
        mine = part[:, pl.ds(pl.multiple_of(base_far + i * R, R), R), :]
        fsum[:, rows, :] = (mine + rfar[0, :, rows, :]) + (rfar[1, :, rows, :] + rfar[2, :, rows, :])
        return carry

    lax.fori_loop(0, 10, far_step, 0)
    pz = remote(fsum, rz, s_pz.at[0], r_pz.at[0], z_dev(zl_n))
    pz.start()
    for cp in near_parts:
        cp.wait_recv()
    base_near = c * (10 * R)

    def near_step(i, carry):
        rows = pl.ds(pl.multiple_of(i * R, R), R)
        mine = part[:, pl.ds(pl.multiple_of(base_near + i * R, R), R), :]
        qsum[:, rows, :] = (mine + rnear[0, :, rows, :]) + (rnear[1, :, rows, :] + rnear[2, :, rows, :])
        return carry

    lax.fori_loop(0, 10, near_step, 0)
    pz.wait_recv()
    for i in range(10):
        rows = slice(i * R, (i + 1) * R)
        qsum[:, rows, :] = qsum[:, rows, :] + rz[:, rows, :]

    q_left = to_left(qsum.at[:, pl.ds(0, R), :], qhalo.at[1], s_q.at[0], r_q.at[1])
    q_right = to_right(qsum.at[:, pl.ds(7 * R, R), :], qhalo.at[0], s_q.at[1], r_q.at[0])
    send_sides([q_left], [q_right])

    @pl.when(has_left)
    def _():
        q_right.wait_recv()

    @pl.when(has_right)
    def _():
        q_left.wait_recv()

    def wide(ref, rows):
        return jnp.concatenate([ref[h, rows, :] for h in range(halves)], axis=1)

    every = slice(0, R)
    qs = [wide(qhalo.at[0], every)]
    qs += [wide(qsum, slice(l * R, (l + 1) * R)) for l in range(R)]
    qs += [wide(qhalo.at[1], every)]
    abs_vec = zero
    for l in range(R):
        v = qs[l + 1]
        before = jnp.where(y_first, wide(qsum, slice(8 * R + l, 8 * R + l + 1)), pltpu.roll(v, 1, 0))
        after = jnp.where(y_last, wide(qsum, slice(9 * R + l, 9 * R + l + 1)), pltpu.roll(v, R - 1, 0))
        value = (
            2.0 * v + qs[l] + qs[l + 2] + before + after
            + jnp.where(z_first, 0.0, z_prev(v)) + jnp.where(z_last, 0.0, z_next(v))
        )
        sens[l] = value
        abs_vec = abs_vec + jnp.abs(value)

    half = abs_vec[:, :128]
    for k in range(1, width // 128):
        half = half + abs_vec[:, k * 128:(k + 1) * 128]
    row = jnp.sum(half, axis=0, keepdims=True)
    sub1 = lax.broadcasted_iota(jnp.int32, (R, 128), 0)
    lane1 = lax.broadcasted_iota(jnp.int32, (R, 128), 1)
    mine_obj = (sub1 == 1) & (lane1 == c)
    now = jnp.where(sub1 == 0, row, jnp.where(mine_obj, obj_part, 0.0))

    stages = [
        (arx, s_ax, r_ax, XC, lambda d: {"case": c, "tile": x_tile(d)}),
        (ary, s_ay, r_ay, YD, lambda d: {"case": y_case(d), "tile": t}),
        (arz, s_az, r_az, z_n, z_dev),
    ]
    all_copies = []
    for i, (buf, ssem, rsem, count, dev) in enumerate(stages):
        msg[i] = now
        copies = []
        for d in range(1, count):
            cp = remote(msg.at[i], buf.at[d - 1], ssem.at[d - 1], rsem.at[d - 1], dev(d))
            cp.start()
            copies.append(cp)
        for cp in copies:
            cp.wait_recv()
        for d in range(1, count):
            now = now + buf[d - 1]
        all_copies += copies

    total_abs = jnp.sum(jnp.where(sub1 == 0, now, 0.0))
    scale = 1.0 / (total_abs / (grid_rows * R * R * width) + 1e-06)
    obj_out[...] = jnp.full(obj_out.shape, jnp.sum(jnp.where(mine_obj, now, 0.0)))
    for l in range(R):
        sens_out[l] = sens[l] * scale

    for cp in [z_copy, pz] + y_copies + yf_copies + far_parts + near_parts + all_copies:
        cp.wait_send()

    @pl.when(has_left)
    def _():
        for cp in [q_left] + halo_left + [left for left, _ in tile_copies]:
            cp.wait_send()

    @pl.when(has_right)
    def _():
        for cp in [q_right] + halo_right + [right for _, right in tile_copies]:
            cp.wait_send()


def body(density, heat_power, laser_mask, sink_mask):
    tiles = lax.axis_size("tile")
    rows, grid_y, width = sink_mask.shape
    planes = (R, R, width)
    halves = width // 128
    f32 = jnp.float32
    z_n = ZH * (tiles // XC)

    def vm(*shape):
        return pltpu.VMEM(shape, f32)

    def dma(*shape):
        return pltpu.SemaphoreType.DMA(shape)

    scratch = [
        vm(EXT, halves, grid_y, 128),
        vm(rows, halves, grid_y, 128),
        pltpu.VMEM((rows, halves, grid_y, 128), jnp.int32),
        pltpu.VMEM((EXT, halves, grid_y, 128), jnp.int32),
        vm(EXT, *planes),
        vm(EXT, *planes),
        vm(EXT, *planes),
    ] + [vm(EXT, *planes)] * 6 + [vm(2, EXT, *planes)] * 3 + [
        vm(halves, 8 * 10 * R, 128),
        vm(YD - 1, halves, 10 * R, 128),
        vm(YD - 1, halves, 10 * R, 128),
        vm(halves, 10 * R, 128),
        vm(halves, 10 * R, 128),
        vm(halves, 10 * R, 128),
        vm(2, halves, R, 128),
        vm(R, R, width),
        vm(3, R, 128),
        vm(XC - 1, R, 128),
        vm(YD - 1, R, 128),
        vm(z_n - 1, R, 128),
        dma(halves, 4),
        dma(YD - 1), dma(YD - 1),
        dma(1), dma(1),
        dma(YD - 1), dma(YD - 1),
        dma(2, 2 * YD), dma(2, 2 * YD),
        dma(4), dma(4),
        dma(2, YD - 1), dma(2, YD - 1),
        dma(1), dma(1),
        dma(2), dma(2),
        dma(XC - 1), dma(XC - 1),
        dma(YD - 1), dma(YD - 1),
        dma(z_n - 1), dma(z_n - 1),
    ]
    any_spec = pl.BlockSpec(memory_space=pl.ANY)
    vmem_spec = pl.BlockSpec(memory_space=pltpu.VMEM)
    sensitivity, objective = pl.pallas_call(
        functools.partial(kernel, tiles),
        out_shape=(
            jax.ShapeDtypeStruct(density.shape, f32),
            jax.ShapeDtypeStruct((1, 128), f32),
        ),
        in_specs=[any_spec] * 4,
        out_specs=(vmem_spec, vmem_spec),
        scratch_shapes=scratch,
        compiler_params=pltpu.CompilerParams(
            collective_id=0, has_side_effects=True, vmem_limit_bytes=48 * 1024 * 1024
        ),
    )(density, heat_power, laser_mask, sink_mask)
    return sensitivity, objective[0, :1]


def solution(mesh):
    return jax.shard_map(
        body,
        mesh=mesh,
        in_specs=(
            P("tile", "case", None),
            P("case", "tile", None, None),
            P("case", "tile", None, None),
            P("tile", None, None),
        ),
        out_specs=(P("tile", "case", None), P("case")),
        check_vma=False,
    )
```

```python
import functools

import jax
import jax.numpy as jnp
from jax import lax
from jax.experimental import pallas as pl
from jax.experimental.pallas import tpu as pltpu
from jax.sharding import PartitionSpec as P

SWEEPS = 6
heat_loss = 0.02
low_cond = 0.01
eig_low = 0.08
eig_high = 2.0

MESH = pl.DeviceIdType.MESH
YD = 4
ZH = 2
XC = 8
R = 8
HL = 4
EXT = 3 * R


def horner_coefficients():
    centre = 0.5 * (eig_high + eig_low)
    half = 0.5 * (eig_high - eig_low)
    ratio = centre / half
    weight = 1.0 / ratio
    x = [1.0 / centre] + [0.0] * (SWEEPS - 1)
    s = list(x)
    for _ in range(1, SWEEPS):
        nxt = 1.0 / (2.0 * ratio - weight)
        r = [-a for a in x]
        r[0] += 1.0
        for k in range(1, SWEEPS):
            r[k] += x[k - 1]
        s = [nxt * weight * a + 2.0 * nxt / half * b for a, b in zip(s, r)]
        x = [a + b for a, b in zip(x, s)]
        weight = nxt
    return x


COEF = horner_coefficients()
LEAD = COEF[-1]


def kernel(
    tiles,
    dens_in, heat_in, laser_in, sink_in,
    sens_out, obj_out,
    dens, relay, heat, laser, sink, src, cond, wgt, kxm, kxp, kym, kyp, kzm, kzp, bias, ya, yb,
    part, rfar, rnear, fsum, rz, qsum, qhalo, sens, msg, arx, arz,
    lsem, round_sem, s_zr, r_zr, s_y, r_y, s_z, r_z, s_yf, r_yf, s_t, r_t, s_tf, r_tf, s_h, r_h, s_p, r_p, s_pz, r_pz, s_q, r_q,
    s_ax, r_ax, s_az, r_az,
):
    zl_n = tiles // XC
    z_n = ZH * zl_n
    c = lax.axis_index("case")
    t = lax.axis_index("tile")
    zh = c // YD
    yy = c % YD
    zl = t // XC
    xc = t % XC
    z = zh * zl_n + zl
    has_left = t > 0
    has_right = t < tiles - 1
    halves = dens.shape[1]
    width = 128 * halves

    def y_case(d):
        return zh * YD + (yy + d) % YD

    def z_dev(d):
        zz = (z + d) % z_n
        return {"case": (zz // zl_n) * YD + yy, "tile": (zz % zl_n) * XC + xc}

    def x_tile(d):
        return zl * XC + (xc + d) % XC

    def plane_dev(k):
        return {"case": y_case(k // XC), "tile": x_tile(k % XC)}

    barrier = pltpu.get_barrier_semaphore()

    def greet(dev):
        pl.semaphore_signal(barrier, inc=1, device_id=dev, device_id_type=MESH)

    met = [z_dev(d) for d in (1, 2, 4, z_n - 1, z_n - 2, z_n - 4)]
    met += [{"case": y_case(d), "tile": t} for d in range(1, YD)]
    met += [{"case": c, "tile": x_tile(d)} for d in range(1, XC)]
    for dev in met:
        greet(dev)

    @pl.when(has_left)
    def _():
        greet({"case": c, "tile": t - 1})

    @pl.when(has_right)
    def _():
        greet({"case": c, "tile": t + 1})

    slab = pl.ds(pl.multiple_of(c * R, R), R)
    loads = []
    for h in range(halves):
        lanes = pl.ds(h * 128, 128)
        loads.append([
            pltpu.make_async_copy(dens_in.at[:, :, lanes], dens.at[pl.ds(R, R), h, slab, :], lsem.at[h, 0]),
            pltpu.make_async_copy(heat_in.at[0, :, :, lanes], heat.at[:, h], lsem.at[h, 1]),
            pltpu.make_async_copy(laser_in.at[0, :, :, lanes], laser.at[:, h], lsem.at[h, 2]),
            pltpu.make_async_copy(sink_in.at[:, :, lanes], sink.at[pl.ds(R, R), h], lsem.at[h, 3]),
        ])
    for k in range(4):
        for h in range(halves):
            loads[h][k].start()

    @pl.when(t == 0)
    def _():
        dens[0:R] = jnp.zeros((R,) + dens.shape[1:], jnp.float32)
        src[2:R] = jnp.zeros((R - 2,) + src.shape[1:], jnp.float32)
        sink[2:R] = jnp.zeros((R - 2,) + sink.shape[1:], jnp.int32)
        qhalo[0] = jnp.zeros(qhalo.shape[1:], jnp.float32)

    @pl.when(t == tiles - 1)
    def _():
        dens[2 * R:] = jnp.zeros((R,) + dens.shape[1:], jnp.float32)
        src[2 * R:3 * R - 2] = jnp.zeros((R - 2,) + src.shape[1:], jnp.float32)
        sink[2 * R:3 * R - 2] = jnp.zeros((R - 2,) + sink.shape[1:], jnp.int32)
        qhalo[1] = jnp.zeros(qhalo.shape[1:], jnp.float32)

    def row_load(ref, l, j):
        return jnp.concatenate([ref[l, h, pl.ds(j, R, stride=R), :] for h in range(halves)], axis=1)

    def make_source(l, carry):
        for j in range(R):
            src[l + R, j] = row_load(heat, l, j) * row_load(laser, l, j).astype(jnp.float32)
        return carry

    pl.semaphore_wait(
        barrier, len(met) + has_left.astype(jnp.int32) + has_right.astype(jnp.int32)
    )

    sends = []

    def drain():
        for guard, group in ((None, []), (has_left, []), (has_right, [])):
            group = [cp for g, cp in sends if g is guard]
            if not group:
                continue

            def wait_all(group=group):
                for cp in group:
                    cp.wait_send()

            if guard is None:
                wait_all()
            else:
                pl.when(guard)(wait_all)

    def push(cp):
        cp.start()
        sends.append((None, cp))
        return cp

    def remote(a, b, ssem, rsem, dev):
        return pltpu.make_async_remote_copy(
            src_ref=a, dst_ref=b, send_sem=ssem, recv_sem=rsem, device_id=dev, device_id_type=MESH
        )

    def to_left(a, b, ssem, rsem):
        return remote(a, b, ssem, rsem, {"case": c, "tile": jnp.maximum(t - 1, 0)})

    def to_right(a, b, ssem, rsem):
        return remote(a, b, ssem, rsem, {"case": c, "tile": jnp.minimum(t + 1, tiles - 1)})

    def piece(base, k, rows):
        return dens.at[pl.ds(base + (k // halves) * HL, HL), k % halves, rows, :]

    def piece_in(k):
        return dens_in.at[pl.ds((k // halves) * HL, HL), :, pl.ds((k % halves) * 128, 128)]

    pieces = halves * R // HL
    quarter = z_n // 4
    column = xc // 2
    via = []
    for k in range(pieces):
        way = quarter if k < pieces // 2 else z_n - quarter
        way = jnp.where(column == 0, quarter, way)
        via.append(jnp.where(column == XC // 2 - 1, z_n - quarter, way))
    for k in range(pieces):
        push(remote(piece_in(k), relay.at[k], s_zr.at[k], r_zr.at[k], z_dev(via[k])))
    y_copies = []
    for d in range(1, YD):
        to = {"case": y_case(d), "tile": t}
        y_copies.append([
            push(remote(piece_in(k), piece(R, k, slab), s_y.at[d - 1, k], r_y.at[d - 1, k], to))
            for k in range(pieces)
        ])

    for dev in met:
        pl.semaphore_signal(round_sem.at[0], inc=1, device_id=dev, device_id_type=MESH)
    for h in range(halves):
        loads[h][3].wait()

    halo_left = [
        to_left(src.at[pl.ds(R, R - 2)], src.at[pl.ds(2 * R, R - 2)], s_h.at[0], r_h.at[1]),
        to_left(sink.at[pl.ds(R, R - 2)], sink.at[pl.ds(2 * R, R - 2)], s_h.at[1], r_h.at[3]),
    ]
    halo_right = [
        to_right(src.at[pl.ds(R + 2, R - 2)], src.at[pl.ds(2, R - 2)], s_h.at[2], r_h.at[0]),
        to_right(sink.at[pl.ds(R + 2, R - 2)], sink.at[pl.ds(2, R - 2)], s_h.at[3], r_h.at[2]),
    ]

    def send_sides(left, right):
        @pl.when(has_left)
        def _():
            for cp in left:
                cp.start()

        @pl.when(has_right)
        def _():
            for cp in right:
                cp.start()

        sends.extend((has_left, cp) for cp in left)
        sends.extend((has_right, cp) for cp in right)

    send_sides(halo_left[1:], halo_right[1:])
    for k in range(3):
        for h in range(halves):
            loads[h][k].wait()
    lax.fori_loop(0, R, make_source, 0)
    send_sides(halo_left[:1], halo_right[:1])

    def slab_of(case):
        return pl.ds(pl.multiple_of(case * R, R), R)

    tile_copies = []

    def forward(case, order):
        rows = slab_of(case)
        here = dens.at[pl.ds(R, R), :, rows, :]
        left = to_left(here, dens.at[pl.ds(2 * R, R), :, rows, :], s_t.at[0, order], r_t.at[1, order])
        right = to_right(here, dens.at[pl.ds(0, R), :, rows, :], s_t.at[1, order], r_t.at[0, order])
        send_sides([left], [right])
        tile_copies.append((left, right))

    def forward_piece(case, order, k):
        rows = slab_of(case)
        here = piece(R, k, rows)
        left = to_left(here, piece(2 * R, k, rows), s_tf.at[0, order, k], r_tf.at[1, order, k])
        right = to_right(here, piece(0, k, rows), s_tf.at[1, order, k], r_tf.at[0, order, k])
        send_sides([left], [right])
        tile_copies.append((left, right))

    forward(c, 0)
    for d in range(1, YD):
        for cp in y_copies[d - 1]:
            cp.wait_recv()
        forward(zh * YD + (yy + YD - d) % YD, d)

    z_copies = []
    for k in range(pieces):
        into = relay.at[k]
        remote(into, into, s_zr.at[k], r_zr.at[k], z_dev(via[k])).wait_recv()
        origin = z_dev(z_n - via[k])["case"]
        z_copies.append(
            push(remote(into, piece(R, k, slab_of(origin)), s_z.at[k], r_z.at[k], z_dev(via[k])))
        )
    pl.semaphore_wait(round_sem.at[0], len(met))
    for dev in met:
        pl.semaphore_signal(round_sem.at[1], inc=1, device_id=dev, device_id_type=MESH)

    far = (1 - zh) * YD
    far_case = far + yy
    yf_copies = []

    def cross(k):
        z_copies[k].wait_recv()
        here = piece(R, k, slab_of(far_case))
        yf_copies.append([
            push(remote(here, here, s_yf.at[d - 1, k], r_yf.at[d - 1, k], {"case": y_case(d), "tile": t}))
            for d in range(1, YD)
        ])
        forward_piece(far_case, 0, k)

    def spread(k):
        for d in range(1, YD):
            yf_copies[k][d - 1].wait_recv()
            forward_piece(far + (yy + YD - d) % YD, d, k)

    for k in range(pieces - 1):
        cross(k)
    spread(0)
    cross(pieces - 1)
    for k in range(1, pieces):
        spread(k)

    @pl.when(has_left)
    def _():
        for left, right in tile_copies:
            right.wait_recv()
        for cp in halo_right:
            cp.wait_recv()

    @pl.when(has_right)
    def _():
        for left, right in tile_copies:
            left.wait_recv()
        for cp in halo_left:
            cp.wait_recv()

    lane = lax.broadcasted_iota(jnp.int32, (R, width), 1)
    sub = lax.broadcasted_iota(jnp.int32, (R, width), 0)
    z_first = lane == 0
    z_last = lane == width - 1
    y_first = sub == 0
    y_last = sub == R - 1
    zero = jnp.zeros((R, width), jnp.float32)
    one = jnp.ones((R, width), jnp.float32)
    grid_rows = tiles * R

    def z_prev(v):
        return pltpu.roll(v, 1, 1)

    def z_next(v):
        return pltpu.roll(v, width - 1, 1)

    lane_h = lax.broadcasted_iota(jnp.int32, (R, 128), 1)

    def z_from_prev(v):
        turned = [pltpu.roll(v[:, h * 128:(h + 1) * 128], 1, 1) for h in range(halves)]
        out = turned[:1] + [jnp.where(lane_h == 0, turned[h - 1], turned[h]) for h in range(1, halves)]
        return jnp.concatenate(out, axis=1)

    def z_from_next(v):
        turned = [pltpu.roll(v[:, h * 128:(h + 1) * 128], 127, 1) for h in range(halves)]
        out = [jnp.where(lane_h == 127, turned[h + 1], turned[h]) for h in range(halves - 1)] + turned[-1:]
        return jnp.concatenate(out, axis=1)

    def around(planes, j):
        before = planes[j - 1] if j > 0 else pltpu.roll(planes[R - 1], 1, 0)
        after = planes[j + 1] if j < R - 1 else pltpu.roll(planes[0], R - 1, 0)
        return before, after

    def flag(cond_):
        return cond_.astype(jnp.float32)

    def physical_step(e, carry):
        g = t * R - R + e
        nx = 2.0 + flag(g > 0) + flag(g < grid_rows - 1)
        nyz = nx + jnp.where(z_first | z_last, 1.0, 2.0)
        planes = [row_load(dens, e, j) for j in range(R)]
        for j in range(R):
            v = planes[j]
            before, after = around(planes, j)
            ny = jnp.full((R, width), 2.0)
            if j == 0:
                before = jnp.where(y_first, 0.0, before)
                ny = jnp.where(y_first, 1.0, 2.0)
            if j == R - 1:
                after = jnp.where(y_last, 0.0, after)
                ny = jnp.where(y_last, 1.0, 2.0)
            total = (
                2.0 * v + row_load(dens, e - 1, j) + row_load(dens, e + 1, j)
                + before + after
                + jnp.where(z_first, 0.0, z_prev(v)) + jnp.where(z_last, 0.0, z_next(v))
            )
            inv = 1.0 / (nyz + ny)
            phys = total * inv
            sq = phys * phys
            cond[e, j] = low_cond + (1.0 - low_cond) * (sq * phys)
            wgt[e, j] = (-1.5 * (1.0 - low_cond) * LEAD * LEAD) * sq * inv
        return carry

    lax.fori_loop(1, EXT - 1, physical_step, 0, unroll=2)

    def inside(g):
        return (g >= 0) & (g < grid_rows)

    def face_step(e, carry):
        g = t * R - R + e
        vm = 0.5 * flag(inside(g - 1) & inside(g))
        vp = 0.5 * flag(inside(g) & inside(g + 1))
        planes = [cond[e, j] for j in range(R)]
        for j in range(R):
            v = planes[j]
            before, after = around(planes, j)
            f_xm = vm * (cond[e - 1, j] + v)
            f_xp = vp * (cond[e + 1, j] + v)
            f_ym = 0.5 * (before + v)
            f_yp = 0.5 * (after + v)
            if j == 0:
                f_ym = jnp.where(y_first, 0.0, f_ym)
            if j == R - 1:
                f_yp = jnp.where(y_last, 0.0, f_yp)
            f_zm = jnp.where(z_first, 0.0, 0.5 * (z_prev(v) + v))
            f_zp = jnp.where(z_last, 0.0, 0.5 * (z_next(v) + v))
            diag = heat_loss + f_xm + f_xp + f_ym + f_yp + f_zm + f_zp
            free = jnp.where(row_load(sink, e, j) == 0, 1.0, 0.0)
            scale = free / diag
            kxm[e, j] = scale * f_xm
            kxp[e, j] = scale * f_xp
            kym[e, j] = scale * f_ym
            kyp[e, j] = scale * f_yp
            kzm[e, j] = scale * f_zm
            kzp[e, j] = scale * f_zp
            source = src[e, j]
            bias[0, e, j] = scale * source
            bias[1, e, j] = jnp.where(source > 0.0, scale, 0.0)
        return carry

    lax.fori_loop(2, EXT - 2, face_step, 0, unroll=2)

    def sweep(n, y_in, y_out):
        ratio = COEF[SWEEPS - 2 - n] / LEAD

        def step(e, carry):
            for j in range(R):
                ks = [k[e, j] for k in (kxm, kxp, kym, kyp, kzm, kzp)]
                for f in range(2):
                    v = y_in[f, e, j]
                    before = y_in[f, e, j - 1] if j > 0 else pltpu.roll(y_in[f, e, R - 1], 1, 0)
                    after = y_in[f, e, j + 1] if j < R - 1 else pltpu.roll(y_in[f, e, 0], R - 1, 0)
                    acc = ratio * bias[f, e, j]
                    acc = acc + ks[0] * y_in[f, e - 1, j]
                    acc = acc + ks[1] * y_in[f, e + 1, j]
                    acc = acc + ks[2] * before
                    acc = acc + ks[3] * after
                    acc = acc + ks[4] * z_from_prev(v)
                    acc = acc + ks[5] * z_from_next(v)
                    y_out[f, e, j] = acc
            return carry

        lax.fori_loop(3 + n, EXT - 3 - n, step, 0, unroll=2)

    bufs = [bias, ya, yb, ya, yb, ya]
    for n in range(SWEEPS - 1):
        sweep(n, bufs[n], bufs[n + 1])
    fin = bufs[SWEEPS - 1]

    def slab_store(row, value):
        for h in range(halves):
            part[h, pl.ds(row, R, stride=10 * R), :] = value[:, h * 128:(h + 1) * 128]

    def product_step(e, total):
        g = t * R - R + e
        l = e - R
        vm = flag(inside(g - 1))
        vp = flag(inside(g + 1))
        ps = [fin[0, e, j] for j in range(R)]
        qs = [fin[1, e, j] for j in range(R)]
        y_faces = []
        for j in range(R):
            pn = around(ps, j)[1]
            qn = around(qs, j)[1]
            face = (ps[j] - pn) * (qs[j] - qn)
            if j == R - 1:
                face = jnp.where(y_last, 0.0, face)
            y_faces.append(face)
        for j in range(R):
            p, q = ps[j], qs[j]
            acc = vm * ((p - fin[0, e - 1, j]) * (q - fin[1, e - 1, j]))
            acc = acc + vp * ((p - fin[0, e + 1, j]) * (q - fin[1, e + 1, j]))
            acc = acc + y_faces[j] + around(y_faces, j)[0]
            face = jnp.where(z_last, 0.0, (p - z_next(p)) * (q - z_next(q)))
            acc = (acc + face + z_prev(face)) * wgt[e, j]
            slab_store(l * R + j, acc)
            if j == R - 1:
                edge = jnp.where(y_first, 0.0, pltpu.roll(acc, 1, 0))
                slab_store(8 * R + l, edge)
            if j == 0:
                edge = jnp.where(y_last, 0.0, pltpu.roll(acc, R - 1, 0))
                slab_store(9 * R + l, edge)
            total = total + jnp.where(src[e, j] > 0.0, p, 0.0)
        return total

    obj_vec = lax.fori_loop(R, 2 * R, product_step, zero, unroll=2)

    def block(case):
        return pl.ds(pl.multiple_of(case * (10 * R), 10 * R), 10 * R)

    def y_parts(side, dest_base, buf):
        return [
            [
                push(remote(
                    part.at[h, block(dest_base + (yy + d) % YD)], buf.at[d - 1, h],
                    s_p.at[side, d - 1, h], r_p.at[side, d - 1, h], {"case": y_case(d), "tile": t},
                ))
                for d in range(1, YD)
            ]
            for h in range(halves)
        ]

    def add_parts(h, case, buf, out):
        base = case * (10 * R)

        def step(i, carry):
            rows = pl.ds(pl.multiple_of(i * R, R), R)
            mine = part[h, pl.ds(pl.multiple_of(base + i * R, R), R), :]
            out[h, rows, :] = (mine + buf[0, h, rows, :]) + (buf[1, h, rows, :] + buf[2, h, rows, :])
            return carry

        lax.fori_loop(0, 10, step, 0, unroll=5)

    far_parts = y_parts(0, far, rfar)
    obj_part = LEAD * jnp.sum(obj_vec, axis=(0, 1), keepdims=True)
    crossing = []
    for h in range(halves):
        for cp in far_parts[h]:
            cp.wait_recv()
        add_parts(h, far_case, rfar, fsum)
        crossing.append(push(remote(fsum.at[h], rz.at[h], s_pz.at[h], r_pz.at[h], z_dev(zl_n))))
    near_parts = y_parts(1, zh * YD, rnear)
    for h in range(halves):
        for cp in near_parts[h]:
            cp.wait_recv()
        add_parts(h, c, rnear, qsum)
    for h in range(halves):
        crossing[h].wait_recv()
        qsum[h] = qsum[h] + rz[h]

    q_left = to_left(qsum.at[:, pl.ds(0, R), :], qhalo.at[1], s_q.at[0], r_q.at[1])
    q_right = to_right(qsum.at[:, pl.ds(7 * R, R), :], qhalo.at[0], s_q.at[1], r_q.at[0])
    send_sides([q_left], [q_right])

    @pl.when(has_left)
    def _():
        q_right.wait_recv()

    @pl.when(has_right)
    def _():
        q_left.wait_recv()

    def wide(ref, rows):
        return jnp.concatenate([ref[h, rows, :] for h in range(halves)], axis=1)

    every = slice(0, R)
    qs = [wide(qhalo.at[0], every)]
    qs += [wide(qsum, slice(l * R, (l + 1) * R)) for l in range(R)]
    qs += [wide(qhalo.at[1], every)]
    abs_vec = zero
    for l in range(R):
        v = qs[l + 1]
        before = jnp.where(y_first, wide(qsum, slice(8 * R + l, 8 * R + l + 1)), pltpu.roll(v, 1, 0))
        after = jnp.where(y_last, wide(qsum, slice(9 * R + l, 9 * R + l + 1)), pltpu.roll(v, R - 1, 0))
        value = (
            2.0 * v + qs[l] + qs[l + 2] + before + after
            + jnp.where(z_first, 0.0, z_prev(v)) + jnp.where(z_last, 0.0, z_next(v))
        )
        sens[l] = value
        abs_vec = abs_vec + jnp.abs(value)

    pl.semaphore_wait(round_sem.at[1], len(met))
    lane1 = lax.broadcasted_iota(jnp.int32, (1, 128), 1)
    now = jnp.where(lane1 == 8, jnp.sum(abs_vec, axis=(0, 1), keepdims=True), jnp.where(lane1 == c, obj_part, 0.0))
    for i, (buf, ssem, rsem, count, dev) in enumerate(
        [(arx, s_ax, r_ax, YD * XC, plane_dev), (arz, s_az, r_az, z_n, z_dev)]
    ):
        msg[i] = now
        copies = [
            push(remote(msg.at[i], buf.at[k - 1], ssem.at[k - 1], rsem.at[k - 1], dev(k))) for k in range(1, count)
        ]
        for cp in copies:
            cp.wait_recv()
        for k in range(1, count):
            now = now + buf[k - 1]

    total_abs = jnp.sum(jnp.where(lane1 == 8, now, 0.0), axis=(0, 1), keepdims=True)
    scale = 1.0 / (total_abs / (grid_rows * R * R * width) + 1e-06)
    obj_out[...] = jnp.zeros_like(obj_out) + jnp.sum(jnp.where(lane1 == c, now, 0.0), axis=(0, 1), keepdims=True)
    for l in range(R):
        sens_out[l] = sens[l] * scale

    drain()


def body(density, heat_power, laser_mask, sink_mask):
    tiles = lax.axis_size("tile")
    rows, grid_y, width = sink_mask.shape
    planes = (R, R, width)
    halves = width // 128
    pieces = halves * R // HL
    f32 = jnp.float32
    z_n = ZH * (tiles // XC)

    def vm(*shape):
        return pltpu.VMEM(shape, f32)

    def dma(*shape):
        return pltpu.SemaphoreType.DMA(shape)

    scratch = [
        vm(EXT, halves, grid_y, 128),
        vm(pieces, HL, R, 128),
        vm(rows, halves, grid_y, 128),
        pltpu.VMEM((rows, halves, grid_y, 128), jnp.int32),
        pltpu.VMEM((EXT, halves, grid_y, 128), jnp.int32),
        vm(EXT, *planes),
        vm(EXT, *planes),
        vm(EXT, *planes),
    ] + [vm(EXT, *planes)] * 6 + [vm(2, EXT, *planes)] * 3 + [
        vm(halves, 8 * 10 * R, 128),
        vm(YD - 1, halves, 10 * R, 128),
        vm(YD - 1, halves, 10 * R, 128),
        vm(halves, 10 * R, 128),
        vm(halves, 10 * R, 128),
        vm(halves, 10 * R, 128),
        vm(2, halves, R, 128),
        vm(R, R, width),
        vm(2, 1, 128),
        vm(YD * XC - 1, 1, 128),
        vm(z_n - 1, 1, 128),
        dma(halves, 4),
        pltpu.SemaphoreType.REGULAR((2,)),
        dma(pieces), dma(pieces),
        dma(YD - 1, pieces), dma(YD - 1, pieces),
        dma(pieces), dma(pieces),
        dma(YD - 1, pieces), dma(YD - 1, pieces),
        dma(2, YD), dma(2, YD),
        dma(2, YD, pieces), dma(2, YD, pieces),
        dma(4), dma(4),
        dma(2, YD - 1, halves), dma(2, YD - 1, halves),
        dma(halves), dma(halves),
        dma(2), dma(2),
        dma(YD * XC - 1), dma(YD * XC - 1),
        dma(z_n - 1), dma(z_n - 1),
    ]
    any_spec = pl.BlockSpec(memory_space=pl.ANY)
    vmem_spec = pl.BlockSpec(memory_space=pltpu.VMEM)
    sensitivity, objective = pl.pallas_call(
        functools.partial(kernel, tiles),
        out_shape=(
            jax.ShapeDtypeStruct(density.shape, f32),
            jax.ShapeDtypeStruct((1, 128), f32),
        ),
        in_specs=[any_spec] * 4,
        out_specs=(vmem_spec, vmem_spec),
        scratch_shapes=scratch,
        compiler_params=pltpu.CompilerParams(
            collective_id=0, has_side_effects=True, vmem_limit_bytes=56150000
        ),
    )(density, heat_power, laser_mask, sink_mask)
    return sensitivity, objective[0, :1]


def solution(mesh):
    return jax.shard_map(
        body,
        mesh=mesh,
        in_specs=(
            P("tile", "case", None),
            P("case", "tile", None, None),
            P("case", "tile", None, None),
            P("tile", None, None),
        ),
        out_specs=(P("tile", "case", None), P("case")),
        check_vma=False,
    )
```

```python
import functools

import jax
import jax.numpy as jnp
from jax import lax
from jax.experimental import pallas as pl
from jax.experimental.pallas import tpu as pltpu
from jax.sharding import PartitionSpec as P

SWEEPS = 6
heat_loss = 0.02
low_cond = 0.01
eig_low = 0.08
eig_high = 2.0

MESH = pl.DeviceIdType.MESH
UNROLL = (6, 4, 7, 6, 5)
YD = 4
ZH = 2
XC = 8
R = 8
HL = 4
RL = 5
EXT = 3 * R


def horner_coefficients():
    centre = 0.5 * (eig_high + eig_low)
    half = 0.5 * (eig_high - eig_low)
    ratio = centre / half
    weight = 1.0 / ratio
    x = [1.0 / centre] + [0.0] * (SWEEPS - 1)
    s = list(x)
    for _ in range(1, SWEEPS):
        nxt = 1.0 / (2.0 * ratio - weight)
        r = [-a for a in x]
        r[0] += 1.0
        for k in range(1, SWEEPS):
            r[k] += x[k - 1]
        s = [nxt * weight * a + 2.0 * nxt / half * b for a, b in zip(s, r)]
        x = [a + b for a, b in zip(x, s)]
        weight = nxt
    return x


COEF = horner_coefficients()
LEAD = COEF[-1]


def kernel(
    tiles,
    dens_in, heat_in, laser_in, sink_in,
    sens_out, obj_out,
    dens, relay, heat, laser, sink, src, wgt, fin, *rest,
):
    near_set, far_set, rest = rest[:12], rest[12:24], rest[24:]
    (
        part, rfar, rnear, fsum, rz, nsum, nhalo, rhalo, sens, msg, arx, arz, lsem, round_sem, s_zr, r_zr, s_y, r_y, s_z, r_z, s_yf, r_yf, s_t, r_t, s_tf, r_tf, s_h, r_h, s_p, r_p, s_pz, r_pz, s_q, r_q, s_ax, r_ax, s_az, r_az,
    ) = rest
    zl_n = tiles // XC
    z_n = ZH * zl_n
    c = lax.axis_index("case")
    t = lax.axis_index("tile")
    zh = c // YD
    yy = c % YD
    zl = t // XC
    xc = t % XC
    z = zh * zl_n + zl
    has_left = t > 0
    has_right = t < tiles - 1
    halves = dens.shape[1]
    width = 128 * halves

    def y_case(d):
        return zh * YD + (yy + d) % YD

    def z_dev(d):
        zz = (z + d) % z_n
        return {"case": (zz // zl_n) * YD + yy, "tile": (zz % zl_n) * XC + xc}

    def x_tile(d):
        return zl * XC + (xc + d) % XC

    def plane_dev(k):
        return {"case": y_case(k // XC), "tile": x_tile(k % XC)}

    barrier = pltpu.get_barrier_semaphore()

    def greet(dev):
        pl.semaphore_signal(barrier, inc=1, device_id=dev, device_id_type=MESH)

    met = [z_dev(d) for d in (1, 2, 4, z_n - 1, z_n - 2, z_n - 4)]
    met += [{"case": y_case(d), "tile": t} for d in range(1, YD)]
    met += [{"case": c, "tile": x_tile(d)} for d in range(1, XC)]
    for dev in met:
        greet(dev)

    @pl.when(has_left)
    def _():
        greet({"case": c, "tile": t - 1})

    @pl.when(has_right)
    def _():
        greet({"case": c, "tile": t + 1})

    slab = pl.ds(pl.multiple_of(c * R, R), R)
    loads = []
    for h in range(halves):
        lanes = pl.ds(h * 128, 128)
        loads.append([
            pltpu.make_async_copy(dens_in.at[:, :, lanes], dens.at[pl.ds(R, R), h, slab, :], lsem.at[h, 0]),
            pltpu.make_async_copy(heat_in.at[0, :, :, lanes], heat.at[:, h], lsem.at[h, 1]),
            pltpu.make_async_copy(laser_in.at[0, :, :, lanes], laser.at[:, h], lsem.at[h, 2]),
            pltpu.make_async_copy(sink_in.at[:, :, lanes], sink.at[pl.ds(R, R), h], lsem.at[h, 3]),
        ])
    for k in range(4):
        for h in range(halves):
            loads[h][k].start()

    @pl.when(t == 0)
    def _():
        dens[0:R] = jnp.zeros((R,) + dens.shape[1:], jnp.float32)
        src[2:R] = jnp.zeros((R - 2,) + src.shape[1:], jnp.float32)
        sink[2:R] = jnp.zeros((R - 2,) + sink.shape[1:], jnp.int32)
        nhalo[0] = jnp.zeros(nhalo.shape[1:], jnp.float32)
        rhalo[0] = jnp.zeros(rhalo.shape[1:], jnp.float32)

    @pl.when(t == tiles - 1)
    def _():
        dens[2 * R:] = jnp.zeros((R,) + dens.shape[1:], jnp.float32)
        src[2 * R:3 * R - 2] = jnp.zeros((R - 2,) + src.shape[1:], jnp.float32)
        sink[2 * R:3 * R - 2] = jnp.zeros((R - 2,) + sink.shape[1:], jnp.int32)
        nhalo[1] = jnp.zeros(nhalo.shape[1:], jnp.float32)
        rhalo[1] = jnp.zeros(rhalo.shape[1:], jnp.float32)

    def make_source(l, carry):
        for j in range(R):
            for h in range(halves):
                rows = pl.ds(j * R, R)
                src[l + R, h, rows, :] = heat[l, h, rows, :] * laser[l, h, rows, :].astype(jnp.float32)
        return carry

    pl.semaphore_wait(
        barrier, len(met) + has_left.astype(jnp.int32) + has_right.astype(jnp.int32)
    )

    sends = []

    def drain():
        for guard, group in ((None, []), (has_left, []), (has_right, [])):
            group = [cp for g, cp in sends if g is guard]
            if not group:
                continue

            def wait_all(group=group):
                for cp in group:
                    cp.wait_send()

            if guard is None:
                wait_all()
            else:
                pl.when(guard)(wait_all)

    def push(cp):
        cp.start()
        sends.append((None, cp))
        return cp

    def remote(a, b, ssem, rsem, dev):
        return pltpu.make_async_remote_copy(
            src_ref=a, dst_ref=b, send_sem=ssem, recv_sem=rsem, device_id=dev, device_id_type=MESH
        )

    def to_left(a, b, ssem, rsem):
        return remote(a, b, ssem, rsem, {"case": c, "tile": jnp.maximum(t - 1, 0)})

    def to_right(a, b, ssem, rsem):
        return remote(a, b, ssem, rsem, {"case": c, "tile": jnp.minimum(t + 1, tiles - 1)})

    def piece(base, k, rows):
        return dens.at[pl.ds(base + (k // halves) * HL, HL), k % halves, rows, :]

    def piece_in(k):
        return dens_in.at[pl.ds((k // halves) * HL, HL), :, pl.ds((k % halves) * 128, 128)]

    pieces = halves * R // HL
    quarter = z_n // 4
    column = xc // 2
    via = []
    for k in range(pieces):
        way = quarter if k < pieces // 2 else z_n - quarter
        way = jnp.where(column == 0, quarter, way)
        via.append(jnp.where(column == XC // 2 - 1, z_n - quarter, way))
    for k in range(pieces):
        push(remote(piece_in(k), relay.at[k], s_zr.at[k], r_zr.at[k], z_dev(via[k])))
    y_copies = []
    for d in range(1, YD):
        to = {"case": y_case(d), "tile": t}
        y_copies.append([
            push(remote(piece_in(k), piece(R, k, slab), s_y.at[d - 1, k], r_y.at[d - 1, k], to))
            for k in range(pieces)
        ])

    for dev in met:
        pl.semaphore_signal(round_sem.at[0], inc=1, device_id=dev, device_id_type=MESH)
    for h in range(halves):
        loads[h][3].wait()

    halo_left = [
        to_left(src.at[pl.ds(R, R - 2)], src.at[pl.ds(2 * R, R - 2)], s_h.at[0], r_h.at[1]),
        to_left(sink.at[pl.ds(R, R - 2)], sink.at[pl.ds(2 * R, R - 2)], s_h.at[1], r_h.at[3]),
    ]
    halo_right = [
        to_right(src.at[pl.ds(R + 2, R - 2)], src.at[pl.ds(2, R - 2)], s_h.at[2], r_h.at[0]),
        to_right(sink.at[pl.ds(R + 2, R - 2)], sink.at[pl.ds(2, R - 2)], s_h.at[3], r_h.at[2]),
    ]

    def send_sides(left, right):
        @pl.when(has_left)
        def _():
            for cp in left:
                cp.start()

        @pl.when(has_right)
        def _():
            for cp in right:
                cp.start()

        sends.extend((has_left, cp) for cp in left)
        sends.extend((has_right, cp) for cp in right)

    send_sides(halo_left[1:], halo_right[1:])
    for k in range(3):
        for h in range(halves):
            loads[h][k].wait()
    lax.fori_loop(0, R, make_source, 0)

    def slab_of(case):
        return pl.ds(pl.multiple_of(case * R, R), R)

    tile_copies = []

    def forward(case, order):
        rows = slab_of(case)
        here = dens.at[pl.ds(R, R), :, rows, :]
        left = to_left(here, dens.at[pl.ds(2 * R, R), :, rows, :], s_t.at[0, order], r_t.at[1, order])
        right = to_right(here, dens.at[pl.ds(0, R), :, rows, :], s_t.at[1, order], r_t.at[0, order])
        send_sides([left], [right])
        tile_copies.append((left, right))

    def forward_piece(case, order, k):
        rows = slab_of(case)
        here = piece(R, k, rows)
        left = to_left(here, piece(2 * R, k, rows), s_tf.at[0, order, k], r_tf.at[1, order, k])
        right = to_right(here, piece(0, k, rows), s_tf.at[1, order, k], r_tf.at[0, order, k])
        send_sides([left], [right])
        tile_copies.append((left, right))

    forward(c, 0)
    for d in range(1, YD):
        for cp in y_copies[d - 1]:
            cp.wait_recv()
        forward(zh * YD + (yy + YD - d) % YD, d)

    send_sides(halo_left[:1], halo_right[:1])

    z_copies = []
    for k in range(pieces):
        into = relay.at[k]
        remote(into, into, s_zr.at[k], r_zr.at[k], z_dev(via[k])).wait_recv()
        origin = z_dev(z_n - via[k])["case"]
        z_copies.append(
            push(remote(into, piece(R, k, slab_of(origin)), s_z.at[k], r_z.at[k], z_dev(via[k])))
        )
    pl.semaphore_wait(round_sem.at[0], len(met))
    for dev in met:
        pl.semaphore_signal(round_sem.at[1], inc=1, device_id=dev, device_id_type=MESH)

    far = (1 - zh) * YD
    far_case = far + yy
    yf_copies = []

    def cross(k):
        z_copies[k].wait_recv()
        here = piece(R, k, slab_of(far_case))
        yf_copies.append({
            d: push(remote(here, here, s_yf.at[d - 1, k], r_yf.at[d - 1, k], {"case": y_case(d), "tile": t}))
            for d in (2, 1, 3)
        })
        forward_piece(far_case, 0, k)

    def spread(k):
        for d in (1, 3, 2):
            yf_copies[k][d].wait_recv()
            forward_piece(far + (yy + YD - d) % YD, d, k)

    for k in range(pieces):
        cross(k)

    def wait_sides(left, right):
        @pl.when(has_left)
        def _():
            for cp in right:
                cp.wait_recv()

        @pl.when(has_right)
        def _():
            for cp in left:
                cp.wait_recv()

    def wait_tiles(pairs):
        wait_sides([left for left, _ in pairs], [right for _, right in pairs])

    lane = lax.broadcasted_iota(jnp.int32, (R, width), 1)
    sub = lax.broadcasted_iota(jnp.int32, (R, width), 0)
    z_first = lane == 0
    z_last = lane == width - 1
    y_first = sub == 0
    y_last = sub == R - 1
    zero = jnp.zeros((R, width), jnp.float32)
    one = jnp.ones((R, width), jnp.float32)
    grid_rows = tiles * R

    def z_prev(v):
        return pltpu.roll(v, 1, 1)

    def z_next(v):
        return pltpu.roll(v, width - 1, 1)

    lane_h = lax.broadcasted_iota(jnp.int32, (R, 128), 1)

    def z_from_prev(v):
        turned = [pltpu.roll(v[:, h * 128:(h + 1) * 128], 1, 1) for h in range(halves)]
        out = turned[:1] + [jnp.where(lane_h == 0, turned[h - 1], turned[h]) for h in range(1, halves)]
        return jnp.concatenate(out, axis=1)

    def z_from_next(v):
        turned = [pltpu.roll(v[:, h * 128:(h + 1) * 128], 127, 1) for h in range(halves)]
        out = [jnp.where(lane_h == 127, turned[h + 1], turned[h]) for h in range(halves - 1)] + turned[-1:]
        return jnp.concatenate(out, axis=1)

    def flag(cond_):
        return cond_.astype(jnp.float32)

    def inside(g):
        return (g >= 0) & (g < grid_rows)

    class Rows:
        def __init__(self, base, count, refs, near=None):
            self.base, self.count, self.near = base, count, near
            self.cond, *self.ks = refs[:7]
            self.ys = refs[7:]
            self.low = 0.0 if near is None else flag(zh == 0)
            self.high = 0.0 if near is None else flag(zh == 1)

        def rows(self, j):
            return pl.ds(self.base + j, R, stride=self.count)

        def load(self, ref, e, j):
            return jnp.concatenate([ref[e, h, self.rows(j), :] for h in range(halves)], axis=1)

        def store(self, ref, e, j, value):
            for h in range(halves):
                ref[e, h, self.rows(j), :] = value[:, h * 128:(h + 1) * 128]

        def around(self, planes, outer=None):
            first = pltpu.roll(planes[-1], 1, 0)
            last = pltpu.roll(planes[0], R - 1, 0)
            if outer is not None:
                first = jnp.where(y_first, outer[0], first)
                last = jnp.where(y_last, outer[1], last)
            return [first] + planes[:-1], planes[1:] + [last]

        def outer(self, get):
            if self.near is None:
                return None
            return get(self.near, YD - 1)[5:6], get(self.near, 0)[2:3]

    def physical_step(e, part_):
        g = t * R - R + e
        nx = 2.0 + flag(g > 0) + flag(g < grid_rows - 1)
        nyz = nx + jnp.where(z_first | z_last, 1.0, 2.0)
        planes = [part_.load(dens, e, j) for j in range(part_.count)]
        outside = None
        if part_.near is not None:
            outside = [
                jnp.concatenate([dens[e, h, y:y + 1, :] for h in range(halves)], axis=1)
                for y in (3 * R - 1, 5 * R)
            ]
        befores, afters = part_.around(planes, outside)
        for j in range(part_.count):
            v, before, after = planes[j], befores[j], afters[j]
            ny = 2.0
            if j == 0:
                has = jnp.where(y_first, part_.low, 1.0)
                before = before * has
                ny = 1.0 + has
            if j == part_.count - 1:
                has = jnp.where(y_last, part_.high, 1.0)
                after = after * has
                ny = 1.0 + has
            total = (
                2.0 * v + part_.load(dens, e - 1, j) + part_.load(dens, e + 1, j) + before + after
                + jnp.where(z_first, 0.0, z_prev(v)) + jnp.where(z_last, 0.0, z_next(v))
            )
            inv = 1.0 / (nyz + ny)
            phys = total * inv
            sq = phys * phys
            part_.cond[e, j] = low_cond + (1.0 - low_cond) * (sq * phys)
            part_.store(wgt, e, j, (-1.5 * (1.0 - low_cond) * LEAD * LEAD) * sq * inv)

    def face_step(e, part_):
        g = t * R - R + e
        vm = 0.5 * flag(inside(g - 1) & inside(g))
        vp = 0.5 * flag(inside(g) & inside(g + 1))
        cond = part_.cond
        planes = [cond[e, j] for j in range(part_.count)]
        befores, afters = part_.around(planes, part_.outer(lambda near, j: near.cond[e, j]))
        for j in range(part_.count):
            v = planes[j]
            f_xm = vm * (cond[e - 1, j] + v)
            f_xp = vp * (cond[e + 1, j] + v)
            f_ym = 0.5 * (befores[j] + v)
            f_yp = 0.5 * (afters[j] + v)
            if j == 0:
                f_ym = f_ym * jnp.where(y_first, part_.low, 1.0)
            if j == part_.count - 1:
                f_yp = f_yp * jnp.where(y_last, part_.high, 1.0)
            f_zm = jnp.where(z_first, 0.0, 0.5 * (z_prev(v) + v))
            f_zp = jnp.where(z_last, 0.0, 0.5 * (z_next(v) + v))
            diag = heat_loss + f_xm + f_xp + f_ym + f_yp + f_zm + f_zp
            free = jnp.where(part_.load(sink, e, j) == 0, 1.0, 0.0)
            scale = free / diag
            for ref, face in zip(part_.ks, (f_xm, f_xp, f_ym, f_yp, f_zm, f_zp)):
                ref[e, j] = scale * face
            source = part_.load(src, e, j)
            part_.ys[0][0, e, j] = scale * source
            part_.ys[0][1, e, j] = jnp.where(source > 0.0, scale, 0.0)

    def sweep_step(n, e, part_):
        ratio = COEF[SWEEPS - 2 - n] / LEAD
        bias, y_in = part_.ys[0], part_.ys[n]
        for f in range(2):
            planes = [y_in[f, e, j] for j in range(part_.count)]
            befores, afters = part_.around(planes, part_.outer(lambda near, j: near.ys[n][f, e, j]))
            for j in range(part_.count):
                ks = [ref[e, j] for ref in part_.ks]
                acc = ratio * bias[f, e, j]
                acc = acc + ks[0] * y_in[f, e - 1, j]
                acc = acc + ks[1] * y_in[f, e + 1, j]
                acc = acc + ks[2] * befores[j]
                acc = acc + ks[3] * afters[j]
                acc = acc + ks[4] * z_from_prev(planes[j])
                acc = acc + ks[5] * z_from_next(planes[j])
                if n == SWEEPS - 2:
                    part_.store(fin.at[f], e, j, acc)
                else:
                    part_.ys[n + 1][f, e, j] = acc

    def over_layers(step, low, high, unroll=1):
        def body(e, carry):
            step(e)
            return carry

        lax.fori_loop(low, high, body, 0, unroll=unroll)

    def set_up_rows(part_):
        over_layers(lambda e: physical_step(e, part_), 1, EXT - 1, 2)

    def solve_rows(part_):
        over_layers(lambda e: face_step(e, part_), 2, EXT - 2, 2)
        for n in range(SWEEPS - 1):
            over_layers(lambda e, n=n: sweep_step(n, e, part_), 3 + n, EXT - 3 - n, UNROLL[n])

    near = Rows(zh * (YD * R), YD, near_set)
    beyond = Rows((1 - zh) * (3 * R), YD + 1, far_set, near)
    wait_tiles(tile_copies[:YD])
    set_up_rows(near)
    for k in range(pieces):
        spread(k)
    wait_sides(halo_left, halo_right)
    solve_rows(near)
    wait_tiles(tile_copies[YD:])
    set_up_rows(beyond)
    solve_rows(beyond)

    def row_load(ref, e, k):
        return jnp.concatenate([ref[e, h, k * R:(k + 1) * R, :] for h in range(halves)], axis=1)

    def slab_store(row, value):
        for h in range(halves):
            part[h, pl.ds(row, value.shape[0]), :] = value[:, h * 128:(h + 1) * 128]

    def product_step(e, total):
        g = t * R - R + e
        l = e - R
        vm = flag(inside(g - 1))
        vp = flag(inside(g + 1))
        ps = [row_load(fin.at[0], e, k) for k in range(R)]
        qs = [row_load(fin.at[1], e, k) for k in range(R)]
        down = []
        for k in range(R):
            up = min(k + 1, R - 1)
            pn = jnp.where(y_last, pltpu.roll(ps[up], R - 1, 0), pltpu.roll(ps[k], R - 1, 0))
            qn = jnp.where(y_last, pltpu.roll(qs[up], R - 1, 0), pltpu.roll(qs[k], R - 1, 0))
            face = (ps[k] - pn) * (qs[k] - qn)
            if k == R - 1:
                face = jnp.where(y_last, 0.0, face)
            down.append((face, pltpu.roll(face, 1, 0)))
        for k in range(R):
            p, q = ps[k], qs[k]
            acc = vm * ((p - row_load(fin.at[0], e - 1, k)) * (q - row_load(fin.at[1], e - 1, k)))
            acc = acc + vp * ((p - row_load(fin.at[0], e + 1, k)) * (q - row_load(fin.at[1], e + 1, k)))
            above = down[k - 1][1] if k > 0 else 0.0
            acc = acc + down[k][0] + jnp.where(y_first, above, down[k][1])
            face = jnp.where(z_last, 0.0, (p - z_next(p)) * (q - z_next(q)))
            acc = (acc + face + z_prev(face)) * row_load(wgt, e, k)
            slab_store(pl.multiple_of(k * 10 * R + l * R, R), acc)
            if k < R - 1:
                slab_store((k + 1) * 10 * R + 8 * R + l, acc[R - 1:])
            if k > 0:
                slab_store((k - 1) * 10 * R + 9 * R + l, acc[:1])
            total = total + jnp.where(row_load(src, e, k) > 0.0, p, 0.0)
        return total

    for h in range(halves):
        part[h, 8 * R:9 * R, :] = jnp.zeros((R, 128), jnp.float32)
        part[h, 7 * 10 * R + 9 * R:7 * 10 * R + 10 * R, :] = jnp.zeros((R, 128), jnp.float32)

    obj_vec = lax.fori_loop(R, R + RL, product_step, zero)

    def part_rows(case, a):
        return pl.ds(pl.multiple_of(case * (10 * R) + a * RL * R, R), RL * R)

    def y_parts(side, dest_base, a, buf):
        rows = pl.ds(a * RL * R, RL * R)
        return [
            [
                push(remote(
                    part.at[h, part_rows(dest_base + (yy + d) % YD, a)], buf.at[d - 1, h, rows],
                    s_p.at[side, d - 1, h, a], r_p.at[side, d - 1, h, a], {"case": y_case(d), "tile": t},
                ))
                for d in range(1, YD)
            ]
            for h in range(halves)
        ]

    def add_parts(h, case, a, buf, out):
        base = case * (10 * R)

        def step(i, carry):
            rows = pl.ds(pl.multiple_of(i * R, R), R)
            mine = part[h, pl.ds(pl.multiple_of(base + i * R, R), R), :]
            out[h, rows, :] = (mine + buf[0, h, rows, :]) + (buf[1, h, rows, :] + buf[2, h, rows, :])
            return carry

        lax.fori_loop(a * RL, (a + 1) * RL, step, 0, unroll=RL)

    far_parts = [y_parts(0, far, 0, rfar)]
    obj_vec = lax.fori_loop(R + RL, 2 * R, product_step, obj_vec)
    far_parts.append(y_parts(0, far, 1, rfar))
    near_parts = [y_parts(1, zh * YD, a, rnear) for a in range(2)]
    obj_part = LEAD * jnp.sum(obj_vec, axis=(0, 1), keepdims=True)

    low = pl.ds(0, R)
    high = pl.ds((R - 1) * R, R)
    left_case = {"case": far_case, "tile": jnp.maximum(t - 1, 0)}
    right_case = {"case": far_case, "tile": jnp.minimum(t + 1, tiles - 1)}
    far_left = remote(fsum.at[:, low], rhalo.at[1], s_q.at[0], r_q.at[1], left_case)
    far_right = remote(fsum.at[:, high], rhalo.at[0], s_q.at[1], r_q.at[0], right_case)
    near_left = to_left(nsum.at[:, low], nhalo.at[1], s_q.at[2], r_q.at[3])
    near_right = to_right(nsum.at[:, high], nhalo.at[0], s_q.at[3], r_q.at[2])
    crossing = []
    for a in range(2):
        rows = pl.ds(a * RL * R, RL * R)
        for h in range(halves):
            for cp in far_parts[a][h]:
                cp.wait_recv()
            add_parts(h, far_case, a, rfar, fsum)
            crossing.append(push(remote(
                fsum.at[h, rows], rz.at[h, rows], s_pz.at[h, a], r_pz.at[h, a], z_dev(zl_n)
            )))
        send_sides([far_left] if a == 0 else [], [] if a == 0 else [far_right])
    for a in range(2):
        for h in range(halves):
            for cp in near_parts[a][h]:
                cp.wait_recv()
            add_parts(h, c, a, rnear, nsum)
    send_sides([near_left], [near_right])
    for cp in crossing:
        cp.wait_recv()

    @pl.when(has_left)
    def _():
        near_right.wait_recv()
        far_right.wait_recv()

    @pl.when(has_right)
    def _():
        near_left.wait_recv()
        far_left.wait_recv()

    def wide(first, second, rows):
        return jnp.concatenate([first[h, rows, :] + second[h, rows, :] for h in range(halves)], axis=1)

    every = slice(0, R)
    qs = [wide(nhalo.at[0], rhalo.at[0], every)]
    qs += [wide(nsum, rz, slice(l * R, (l + 1) * R)) for l in range(R)]
    qs += [wide(nhalo.at[1], rhalo.at[1], every)]
    abs_vec = zero
    for l in range(R):
        v = qs[l + 1]
        before = jnp.where(y_first, wide(nsum, rz, slice(8 * R + l, 8 * R + l + 1)), pltpu.roll(v, 1, 0))
        after = jnp.where(y_last, wide(nsum, rz, slice(9 * R + l, 9 * R + l + 1)), pltpu.roll(v, R - 1, 0))
        value = (
            2.0 * v + qs[l] + qs[l + 2] + before + after
            + jnp.where(z_first, 0.0, z_prev(v)) + jnp.where(z_last, 0.0, z_next(v))
        )
        sens[l] = value
        abs_vec = abs_vec + jnp.abs(value)

    pl.semaphore_wait(round_sem.at[1], len(met))
    lane1 = lax.broadcasted_iota(jnp.int32, (1, 128), 1)
    now = jnp.where(lane1 == 8, jnp.sum(abs_vec, axis=(0, 1), keepdims=True), jnp.where(lane1 == c, obj_part, 0.0))
    for i, (buf, ssem, rsem, count, dev) in enumerate(
        [(arx, s_ax, r_ax, YD * XC, plane_dev), (arz, s_az, r_az, z_n, z_dev)]
    ):
        msg[i] = now
        before = list(sends)
        copies = [
            push(remote(msg.at[i], buf.at[k - 1], ssem.at[k - 1], rsem.at[k - 1], dev(k))) for k in range(1, count)
        ]
        if i == 1:
            sends[:] = before
            drain()
            sends[:] = [(None, cp) for cp in copies]
        for cp in copies:
            cp.wait_recv()
        for k in range(1, count):
            now = now + buf[k - 1]

    total_abs = jnp.sum(jnp.where(lane1 == 8, now, 0.0), axis=(0, 1), keepdims=True)
    scale = 1.0 / (total_abs / (grid_rows * R * R * width) + 1e-06)
    obj_out[...] = jnp.zeros_like(obj_out) + jnp.sum(jnp.where(lane1 == c, now, 0.0), axis=(0, 1), keepdims=True)
    for l in range(R):
        sens_out[l] = sens[l] * scale

    drain()


def body(density, heat_power, laser_mask, sink_mask):
    tiles = lax.axis_size("tile")
    rows, grid_y, width = sink_mask.shape
    halves = width // 128
    pieces = halves * R // HL
    f32 = jnp.float32
    z_n = ZH * (tiles // XC)

    def vm(*shape):
        return pltpu.VMEM(shape, f32)

    def dma(*shape):
        return pltpu.SemaphoreType.DMA(shape)

    scratch = [
        vm(EXT, halves, grid_y, 128),
        vm(pieces, HL, R, 128),
        vm(rows, halves, grid_y, 128),
        pltpu.VMEM((rows, halves, grid_y, 128), jnp.int32),
        pltpu.VMEM((EXT, halves, grid_y, 128), jnp.int32),
        vm(EXT, halves, grid_y, 128),
        vm(EXT, halves, grid_y, 128),
        vm(2, EXT, halves, grid_y, 128),
    ]
    for count in (YD, YD + 1):
        scratch += [vm(EXT, count, R, width)] * 7 + [vm(2, EXT, count, R, width)] * (SWEEPS - 1)
    scratch += [
        vm(halves, 8 * 10 * R, 128),
        vm(YD - 1, halves, 10 * R, 128),
        vm(YD - 1, halves, 10 * R, 128),
        vm(halves, 10 * R, 128),
        vm(halves, 10 * R, 128),
        vm(halves, 10 * R, 128),
        vm(2, halves, R, 128),
        vm(2, halves, R, 128),
        vm(R, R, width),
        vm(2, 1, 128),
        vm(YD * XC - 1, 1, 128),
        vm(z_n - 1, 1, 128),
        dma(halves, 4),
        pltpu.SemaphoreType.REGULAR((2,)),
        dma(pieces), dma(pieces),
        dma(YD - 1, pieces), dma(YD - 1, pieces),
        dma(pieces), dma(pieces),
        dma(YD - 1, pieces), dma(YD - 1, pieces),
        dma(2, YD), dma(2, YD),
        dma(2, YD, pieces), dma(2, YD, pieces),
        dma(4), dma(4),
        dma(2, YD - 1, halves, 2), dma(2, YD - 1, halves, 2),
        dma(halves, 2), dma(halves, 2),
        dma(4), dma(4),
        dma(YD * XC - 1), dma(YD * XC - 1),
        dma(z_n - 1), dma(z_n - 1),
    ]
    any_spec = pl.BlockSpec(memory_space=pl.ANY)
    vmem_spec = pl.BlockSpec(memory_space=pltpu.VMEM)
    sensitivity, objective = pl.pallas_call(
        functools.partial(kernel, tiles),
        out_shape=(
            jax.ShapeDtypeStruct(density.shape, f32),
            jax.ShapeDtypeStruct((1, 128), f32),
        ),
        in_specs=[any_spec] * 4,
        out_specs=(vmem_spec, vmem_spec),
        scratch_shapes=scratch,
        compiler_params=pltpu.CompilerParams(
            collective_id=0, has_side_effects=True, vmem_limit_bytes=56150000
        ),
    )(density, heat_power, laser_mask, sink_mask)
    return sensitivity, objective[0, :1]


def solution(mesh):
    return jax.shard_map(
        body,
        mesh=mesh,
        in_specs=(
            P("tile", "case", None),
            P("case", "tile", None, None),
            P("case", "tile", None, None),
            P("tile", None, None),
        ),
        out_specs=(P("tile", "case", None), P("case")),
        check_vma=False,
    )
```

```python
import functools

import jax
import jax.numpy as jnp
from jax import lax
from jax.experimental import pallas as pl
from jax.experimental.pallas import tpu as pltpu
from jax.sharding import PartitionSpec as P

SWEEPS = 6
heat_loss = 0.02
low_cond = 0.01
eig_low = 0.08
eig_high = 2.0

MESH = pl.DeviceIdType.MESH
UNROLL = (6, 4, 7, 6, 5)
YD = 4
ZH = 2
XC = 8
R = 8
HL = 4
RL = 5
EXT = 3 * R


def horner_coefficients():
    centre = 0.5 * (eig_high + eig_low)
    half = 0.5 * (eig_high - eig_low)
    ratio = centre / half
    weight = 1.0 / ratio
    x = [1.0 / centre] + [0.0] * (SWEEPS - 1)
    s = list(x)
    for _ in range(1, SWEEPS):
        nxt = 1.0 / (2.0 * ratio - weight)
        r = [-a for a in x]
        r[0] += 1.0
        for k in range(1, SWEEPS):
            r[k] += x[k - 1]
        s = [nxt * weight * a + 2.0 * nxt / half * b for a, b in zip(s, r)]
        x = [a + b for a, b in zip(x, s)]
        weight = nxt
    return x


COEF = horner_coefficients()
LEAD = COEF[-1]


def kernel(
    tiles,
    dens_in, heat_in, laser_in, sink_in,
    sens_out, obj_out,
    dens, relay, heat, laser, sink, src, wgt, fin, *rest,
):
    near_set, far_set, rest = rest[:12], rest[12:24], rest[24:]
    (
        part, rfar, rnear, fsum, rz, nsum, nhalo, rhalo, sens, msg, arx, arz, lsem, round_sem, s_zr, r_zr, s_y, r_y, s_z, r_z, s_yf, r_yf, s_t, r_t, s_tf, r_tf, s_h, r_h, s_p, r_p, s_pz, r_pz, s_q, r_q, s_ax, r_ax, s_az, r_az,
    ) = rest
    zl_n = tiles // XC
    z_n = ZH * zl_n
    c = lax.axis_index("case")
    t = lax.axis_index("tile")
    zh = c // YD
    yy = c % YD
    zl = t // XC
    xc = t % XC
    z = zh * zl_n + zl
    has_left = t > 0
    has_right = t < tiles - 1
    halves = dens.shape[1]
    width = 128 * halves

    def y_case(d):
        return zh * YD + (yy + d) % YD

    def z_dev(d):
        zz = (z + d) % z_n
        return {"case": (zz // zl_n) * YD + yy, "tile": (zz % zl_n) * XC + xc}

    def x_tile(d):
        return zl * XC + (xc + d) % XC

    def plane_dev(k):
        return {"case": y_case(k // XC), "tile": x_tile(k % XC)}

    barrier = pltpu.get_barrier_semaphore()

    def greet(dev):
        pl.semaphore_signal(barrier, inc=1, device_id=dev, device_id_type=MESH)

    met = [z_dev(d) for d in (1, 2, 4, z_n - 1, z_n - 2, z_n - 4)]
    met += [{"case": y_case(d), "tile": t} for d in range(1, YD)]
    met += [{"case": c, "tile": x_tile(d)} for d in range(1, XC)]
    for dev in met:
        greet(dev)

    @pl.when(has_left)
    def _():
        greet({"case": c, "tile": t - 1})

    @pl.when(has_right)
    def _():
        greet({"case": c, "tile": t + 1})

    slab = pl.ds(pl.multiple_of(c * R, R), R)
    loads = []
    for h in range(halves):
        lanes = pl.ds(h * 128, 128)
        loads.append([
            pltpu.make_async_copy(dens_in.at[:, :, lanes], dens.at[pl.ds(R, R), h, slab, :], lsem.at[h, 0]),
            pltpu.make_async_copy(heat_in.at[0, :, :, lanes], heat.at[:, h], lsem.at[h, 1]),
            pltpu.make_async_copy(laser_in.at[0, :, :, lanes], laser.at[:, h], lsem.at[h, 2]),
            pltpu.make_async_copy(sink_in.at[:, :, lanes], sink.at[pl.ds(R, R), h], lsem.at[h, 3]),
        ])
    for k in range(4):
        for h in range(halves):
            loads[h][k].start()

    @pl.when(t == 0)
    def _():
        dens[0:R] = jnp.zeros((R,) + dens.shape[1:], jnp.float32)
        src[2:R] = jnp.zeros((R - 2,) + src.shape[1:], jnp.float32)
        sink[2:R] = jnp.zeros((R - 2,) + sink.shape[1:], jnp.int32)
        nhalo[0] = jnp.zeros(nhalo.shape[1:], jnp.float32)
        rhalo[0] = jnp.zeros(rhalo.shape[1:], jnp.float32)

    @pl.when(t == tiles - 1)
    def _():
        dens[2 * R:] = jnp.zeros((R,) + dens.shape[1:], jnp.float32)
        src[2 * R:3 * R - 2] = jnp.zeros((R - 2,) + src.shape[1:], jnp.float32)
        sink[2 * R:3 * R - 2] = jnp.zeros((R - 2,) + sink.shape[1:], jnp.int32)
        nhalo[1] = jnp.zeros(nhalo.shape[1:], jnp.float32)
        rhalo[1] = jnp.zeros(rhalo.shape[1:], jnp.float32)

    def make_source(l, carry):
        for j in range(R):
            for h in range(halves):
                rows = pl.ds(j * R, R)
                src[l + R, h, rows, :] = heat[l, h, rows, :] * laser[l, h, rows, :].astype(jnp.float32)
        return carry

    pl.semaphore_wait(
        barrier, len(met) + has_left.astype(jnp.int32) + has_right.astype(jnp.int32)
    )

    sends = []

    def drain():
        for guard, group in ((None, []), (has_left, []), (has_right, [])):
            group = [cp for g, cp in sends if g is guard]
            if not group:
                continue

            def wait_all(group=group):
                for cp in group:
                    cp.wait_send()

            if guard is None:
                wait_all()
            else:
                pl.when(guard)(wait_all)

    def push(cp):
        cp.start()
        sends.append((None, cp))
        return cp

    def remote(a, b, ssem, rsem, dev):
        return pltpu.make_async_remote_copy(
            src_ref=a, dst_ref=b, send_sem=ssem, recv_sem=rsem, device_id=dev, device_id_type=MESH
        )

    def to_left(a, b, ssem, rsem):
        return remote(a, b, ssem, rsem, {"case": c, "tile": jnp.maximum(t - 1, 0)})

    def to_right(a, b, ssem, rsem):
        return remote(a, b, ssem, rsem, {"case": c, "tile": jnp.minimum(t + 1, tiles - 1)})

    def piece(base, k, rows):
        return dens.at[pl.ds(base + (k // halves) * HL, HL), k % halves, rows, :]

    def piece_in(k):
        return dens_in.at[pl.ds((k // halves) * HL, HL), :, pl.ds((k % halves) * 128, 128)]

    pieces = halves * R // HL
    quarter = z_n // 4
    column = xc // 2
    via = []
    for k in range(pieces):
        way = quarter if k < pieces // 2 else z_n - quarter
        if k < pieces - 1:
            way = jnp.where(column == 0, quarter, way)
        if k > 0:
            way = jnp.where(column == XC // 2 - 1, z_n - quarter, way)
        via.append(way)
    for k in range(pieces):
        push(remote(piece_in(k), relay.at[k], s_zr.at[k], r_zr.at[k], z_dev(via[k])))
    y_copies = []
    for d in range(1, YD):
        to = {"case": y_case(d), "tile": t}
        y_copies.append([
            push(remote(piece_in(k), piece(R, k, slab), s_y.at[d - 1, k], r_y.at[d - 1, k], to))
            for k in range(pieces)
        ])

    for dev in met:
        pl.semaphore_signal(round_sem.at[0], inc=1, device_id=dev, device_id_type=MESH)
    for h in range(halves):
        loads[h][3].wait()

    halo_left = [
        to_left(src.at[pl.ds(R, R - 2)], src.at[pl.ds(2 * R, R - 2)], s_h.at[0], r_h.at[1]),
        to_left(sink.at[pl.ds(R, R - 2)], sink.at[pl.ds(2 * R, R - 2)], s_h.at[1], r_h.at[3]),
    ]
    halo_right = [
        to_right(src.at[pl.ds(R + 2, R - 2)], src.at[pl.ds(2, R - 2)], s_h.at[2], r_h.at[0]),
        to_right(sink.at[pl.ds(R + 2, R - 2)], sink.at[pl.ds(2, R - 2)], s_h.at[3], r_h.at[2]),
    ]

    def send_sides(left, right):
        @pl.when(has_left)
        def _():
            for cp in left:
                cp.start()

        @pl.when(has_right)
        def _():
            for cp in right:
                cp.start()

        sends.extend((has_left, cp) for cp in left)
        sends.extend((has_right, cp) for cp in right)

    send_sides(halo_left[1:], halo_right[1:])
    for k in range(3):
        for h in range(halves):
            loads[h][k].wait()
    lax.fori_loop(0, R, make_source, 0)

    def slab_of(case):
        return pl.ds(pl.multiple_of(case * R, R), R)

    tile_copies = []

    def forward(case, order):
        rows = slab_of(case)
        here = dens.at[pl.ds(R, R), :, rows, :]
        left = to_left(here, dens.at[pl.ds(2 * R, R), :, rows, :], s_t.at[0, order], r_t.at[1, order])
        right = to_right(here, dens.at[pl.ds(0, R), :, rows, :], s_t.at[1, order], r_t.at[0, order])
        send_sides([left], [right])
        tile_copies.append((left, right))

    def forward_piece(case, order, k):
        rows = slab_of(case)
        here = piece(R, k, rows)
        left = to_left(here, piece(2 * R, k, rows), s_tf.at[0, order, k], r_tf.at[1, order, k])
        right = to_right(here, piece(0, k, rows), s_tf.at[1, order, k], r_tf.at[0, order, k])
        send_sides([left], [right])
        tile_copies.append((left, right))

    forward(c, 0)
    for d in range(1, YD):
        for cp in y_copies[d - 1]:
            cp.wait_recv()
        forward(zh * YD + (yy + YD - d) % YD, d)

    send_sides(halo_left[:1], halo_right[:1])

    z_copies = []
    for k in range(pieces):
        into = relay.at[k]
        remote(into, into, s_zr.at[k], r_zr.at[k], z_dev(via[k])).wait_recv()
        origin = z_dev(z_n - via[k])["case"]
        z_copies.append(
            push(remote(into, piece(R, k, slab_of(origin)), s_z.at[k], r_z.at[k], z_dev(via[k])))
        )
    pl.semaphore_wait(round_sem.at[0], len(met))
    for dev in met:
        pl.semaphore_signal(round_sem.at[1], inc=1, device_id=dev, device_id_type=MESH)

    far = (1 - zh) * YD
    far_case = far + yy
    yf_copies = []

    def cross(k):
        z_copies[k].wait_recv()
        here = piece(R, k, slab_of(far_case))
        yf_copies.append({
            d: push(remote(here, here, s_yf.at[d - 1, k], r_yf.at[d - 1, k], {"case": y_case(d), "tile": t}))
            for d in (2, 1, 3)
        })
        forward_piece(far_case, 0, k)

    def spread(k):
        for d in (1, 3, 2):
            yf_copies[k][d].wait_recv()
            forward_piece(far + (yy + YD - d) % YD, d, k)

    for k in range(pieces):
        cross(k)

    def wait_sides(left, right):
        @pl.when(has_left)
        def _():
            for cp in right:
                cp.wait_recv()

        @pl.when(has_right)
        def _():
            for cp in left:
                cp.wait_recv()

    def wait_tiles(pairs):
        wait_sides([left for left, _ in pairs], [right for _, right in pairs])

    lane = lax.broadcasted_iota(jnp.int32, (R, width), 1)
    sub = lax.broadcasted_iota(jnp.int32, (R, width), 0)
    z_first = lane == 0
    z_last = lane == width - 1
    y_first = sub == 0
    y_last = sub == R - 1
    zero = jnp.zeros((R, width), jnp.float32)
    one = jnp.ones((R, width), jnp.float32)
    grid_rows = tiles * R

    def z_prev(v):
        return pltpu.roll(v, 1, 1)

    def z_next(v):
        return pltpu.roll(v, width - 1, 1)

    lane_h = lax.broadcasted_iota(jnp.int32, (R, 128), 1)

    def z_from_prev(v):
        turned = [pltpu.roll(v[:, h * 128:(h + 1) * 128], 1, 1) for h in range(halves)]
        out = turned[:1] + [jnp.where(lane_h == 0, turned[h - 1], turned[h]) for h in range(1, halves)]
        return jnp.concatenate(out, axis=1)

    def z_from_next(v):
        turned = [pltpu.roll(v[:, h * 128:(h + 1) * 128], 127, 1) for h in range(halves)]
        out = [jnp.where(lane_h == 127, turned[h + 1], turned[h]) for h in range(halves - 1)] + turned[-1:]
        return jnp.concatenate(out, axis=1)

    def flag(cond_):
        return cond_.astype(jnp.float32)

    def inside(g):
        return (g >= 0) & (g < grid_rows)

    class Rows:
        def __init__(self, base, count, refs, near=None):
            self.base, self.count, self.near = base, count, near
            self.cond, *self.ks = refs[:7]
            self.ys = refs[7:]
            self.low = 0.0 if near is None else flag(zh == 0)
            self.high = 0.0 if near is None else flag(zh == 1)

        def rows(self, j):
            return pl.ds(self.base + j, R, stride=self.count)

        def load(self, ref, e, j):
            return jnp.concatenate([ref[e, h, self.rows(j), :] for h in range(halves)], axis=1)

        def store(self, ref, e, j, value):
            for h in range(halves):
                ref[e, h, self.rows(j), :] = value[:, h * 128:(h + 1) * 128]

        def around(self, planes, outer=None):
            first = pltpu.roll(planes[-1], 1, 0)
            last = pltpu.roll(planes[0], R - 1, 0)
            if outer is not None:
                first = jnp.where(y_first, outer[0], first)
                last = jnp.where(y_last, outer[1], last)
            return [first] + planes[:-1], planes[1:] + [last]

        def outer(self, get):
            if self.near is None:
                return None
            return get(self.near, YD - 1)[5:6], get(self.near, 0)[2:3]

    def physical_step(e, part_):
        g = t * R - R + e
        nx = 2.0 + flag(g > 0) + flag(g < grid_rows - 1)
        nyz = nx + jnp.where(z_first | z_last, 1.0, 2.0)
        planes = [part_.load(dens, e, j) for j in range(part_.count)]
        outside = None
        if part_.near is not None:
            outside = [
                jnp.concatenate([dens[e, h, y:y + 1, :] for h in range(halves)], axis=1)
                for y in (3 * R - 1, 5 * R)
            ]
        befores, afters = part_.around(planes, outside)
        for j in range(part_.count):
            v, before, after = planes[j], befores[j], afters[j]
            ny = 2.0
            if j == 0:
                has = jnp.where(y_first, part_.low, 1.0)
                before = before * has
                ny = 1.0 + has
            if j == part_.count - 1:
                has = jnp.where(y_last, part_.high, 1.0)
                after = after * has
                ny = 1.0 + has
            total = (
                2.0 * v + part_.load(dens, e - 1, j) + part_.load(dens, e + 1, j) + before + after
                + jnp.where(z_first, 0.0, z_prev(v)) + jnp.where(z_last, 0.0, z_next(v))
            )
            inv = 1.0 / (nyz + ny)
            phys = total * inv
            sq = phys * phys
            part_.cond[e, j] = low_cond + (1.0 - low_cond) * (sq * phys)
            part_.store(wgt, e, j, (-1.5 * (1.0 - low_cond) * LEAD * LEAD) * sq * inv)

    def face_step(e, part_):
        g = t * R - R + e
        vm = 0.5 * flag(inside(g - 1) & inside(g))
        vp = 0.5 * flag(inside(g) & inside(g + 1))
        cond = part_.cond
        planes = [cond[e, j] for j in range(part_.count)]
        befores, afters = part_.around(planes, part_.outer(lambda near, j: near.cond[e, j]))
        for j in range(part_.count):
            v = planes[j]
            f_xm = vm * (cond[e - 1, j] + v)
            f_xp = vp * (cond[e + 1, j] + v)
            f_ym = 0.5 * (befores[j] + v)
            f_yp = 0.5 * (afters[j] + v)
            if j == 0:
                f_ym = f_ym * jnp.where(y_first, part_.low, 1.0)
            if j == part_.count - 1:
                f_yp = f_yp * jnp.where(y_last, part_.high, 1.0)
            f_zm = jnp.where(z_first, 0.0, 0.5 * (z_prev(v) + v))
            f_zp = jnp.where(z_last, 0.0, 0.5 * (z_next(v) + v))
            diag = heat_loss + f_xm + f_xp + f_ym + f_yp + f_zm + f_zp
            free = jnp.where(part_.load(sink, e, j) == 0, 1.0, 0.0)
            scale = free / diag
            for ref, face in zip(part_.ks, (f_xm, f_xp, f_ym, f_yp, f_zm, f_zp)):
                ref[e, j] = scale * face
            source = part_.load(src, e, j)
            part_.ys[0][0, e, j] = scale * source
            part_.ys[0][1, e, j] = jnp.where(source > 0.0, scale, 0.0)

    def sweep_step(n, e, part_):
        ratio = COEF[SWEEPS - 2 - n] / LEAD
        bias, y_in = part_.ys[0], part_.ys[n]
        for f in range(2):
            planes = [y_in[f, e, j] for j in range(part_.count)]
            befores, afters = part_.around(planes, part_.outer(lambda near, j: near.ys[n][f, e, j]))
            for j in range(part_.count):
                ks = [ref[e, j] for ref in part_.ks]
                acc = ratio * bias[f, e, j]
                acc = acc + ks[0] * y_in[f, e - 1, j]
                acc = acc + ks[1] * y_in[f, e + 1, j]
                acc = acc + ks[2] * befores[j]
                acc = acc + ks[3] * afters[j]
                acc = acc + ks[4] * z_from_prev(planes[j])
                acc = acc + ks[5] * z_from_next(planes[j])
                if n == SWEEPS - 2:
                    part_.store(fin.at[f], e, j, acc)
                else:
                    part_.ys[n + 1][f, e, j] = acc

    def over_layers(step, low, high, unroll=1):
        def body(e, carry):
            step(e)
            return carry

        lax.fori_loop(low, high, body, 0, unroll=unroll)

    def set_up_rows(part_, low=1, high=EXT - 1):
        over_layers(lambda e: physical_step(e, part_), low, high, 2)

    def face_rows(part_, low=2, high=EXT - 2):
        over_layers(lambda e: face_step(e, part_), low, high, 2)

    def solve_rows(part_):
        for n in range(SWEEPS - 1):
            over_layers(lambda e, n=n: sweep_step(n, e, part_), 3 + n, EXT - 3 - n, UNROLL[n])

    near = Rows(zh * (YD * R), YD, near_set)
    beyond = Rows((1 - zh) * (3 * R), YD + 1, far_set, near)
    wait_tiles(tile_copies[:YD])
    set_up_rows(near)
    for k in range(pieces):
        spread(k)
    wait_sides(halo_left, halo_right)
    face_rows(near)
    solve_rows(near)
    set_up_rows(beyond, R + 1, 2 * R - 1)
    face_rows(beyond, R + 2, 2 * R - 2)
    wait_tiles(tile_copies[YD:])
    set_up_rows(beyond, 1, R + 1)
    set_up_rows(beyond, 2 * R - 1, EXT - 1)
    face_rows(beyond, 2, R + 2)
    face_rows(beyond, 2 * R - 2, EXT - 2)
    solve_rows(beyond)

    def row_load(ref, e, k):
        return jnp.concatenate([ref[e, h, k * R:(k + 1) * R, :] for h in range(halves)], axis=1)

    def slab_store(row, value):
        for h in range(halves):
            part[h, pl.ds(row, value.shape[0]), :] = value[:, h * 128:(h + 1) * 128]

    def product_step(e, total):
        g = t * R - R + e
        l = e - R
        vm = flag(inside(g - 1))
        vp = flag(inside(g + 1))
        ps = [row_load(fin.at[0], e, k) for k in range(R)]
        qs = [row_load(fin.at[1], e, k) for k in range(R)]
        down = []
        for k in range(R):
            up = min(k + 1, R - 1)
            pn = jnp.where(y_last, pltpu.roll(ps[up], R - 1, 0), pltpu.roll(ps[k], R - 1, 0))
            qn = jnp.where(y_last, pltpu.roll(qs[up], R - 1, 0), pltpu.roll(qs[k], R - 1, 0))
            face = (ps[k] - pn) * (qs[k] - qn)
            if k == R - 1:
                face = jnp.where(y_last, 0.0, face)
            down.append((face, pltpu.roll(face, 1, 0)))
        for k in range(R):
            p, q = ps[k], qs[k]
            acc = vm * ((p - row_load(fin.at[0], e - 1, k)) * (q - row_load(fin.at[1], e - 1, k)))
            acc = acc + vp * ((p - row_load(fin.at[0], e + 1, k)) * (q - row_load(fin.at[1], e + 1, k)))
            above = down[k - 1][1] if k > 0 else 0.0
            acc = acc + down[k][0] + jnp.where(y_first, above, down[k][1])
            face = jnp.where(z_last, 0.0, (p - z_next(p)) * (q - z_next(q)))
            acc = (acc + face + z_prev(face)) * row_load(wgt, e, k)
            slab_store(pl.multiple_of(k * 10 * R + l * R, R), acc)
            if k < R - 1:
                slab_store((k + 1) * 10 * R + 8 * R + l, acc[R - 1:])
            if k > 0:
                slab_store((k - 1) * 10 * R + 9 * R + l, acc[:1])
            total = total + jnp.where(row_load(src, e, k) > 0.0, p, 0.0)
        return total

    for h in range(halves):
        part[h, 8 * R:9 * R, :] = jnp.zeros((R, 128), jnp.float32)
        part[h, 7 * 10 * R + 9 * R:7 * 10 * R + 10 * R, :] = jnp.zeros((R, 128), jnp.float32)

    obj_vec = lax.fori_loop(R, R + RL, product_step, zero)

    def part_rows(case, a):
        return pl.ds(pl.multiple_of(case * (10 * R) + a * RL * R, R), RL * R)

    def y_parts(side, dest_base, a, buf):
        rows = pl.ds(a * RL * R, RL * R)
        return [
            [
                push(remote(
                    part.at[h, part_rows(dest_base + (yy + d) % YD, a)], buf.at[d - 1, h, rows],
                    s_p.at[side, d - 1, h, a], r_p.at[side, d - 1, h, a], {"case": y_case(d), "tile": t},
                ))
                for d in range(1, YD)
            ]
            for h in range(halves)
        ]

    def add_parts(h, case, a, buf, out):
        base = case * (10 * R)

        def step(i, carry):
            rows = pl.ds(pl.multiple_of(i * R, R), R)
            mine = part[h, pl.ds(pl.multiple_of(base + i * R, R), R), :]
            out[h, rows, :] = (mine + buf[0, h, rows, :]) + (buf[1, h, rows, :] + buf[2, h, rows, :])
            return carry

        lax.fori_loop(a * RL, (a + 1) * RL, step, 0, unroll=RL)

    far_parts = [y_parts(0, far, 0, rfar)]
    obj_vec = lax.fori_loop(R + RL, 2 * R, product_step, obj_vec)
    far_parts.append(y_parts(0, far, 1, rfar))
    near_parts = [y_parts(1, zh * YD, a, rnear) for a in range(2)]
    obj_part = LEAD * jnp.sum(obj_vec, axis=(0, 1), keepdims=True)

    low = pl.ds(0, R)
    high = pl.ds((R - 1) * R, R)
    left_case = {"case": far_case, "tile": jnp.maximum(t - 1, 0)}
    right_case = {"case": far_case, "tile": jnp.minimum(t + 1, tiles - 1)}
    far_left = remote(fsum.at[:, low], rhalo.at[1], s_q.at[0], r_q.at[1], left_case)
    far_right = remote(fsum.at[:, high], rhalo.at[0], s_q.at[1], r_q.at[0], right_case)
    near_left = to_left(nsum.at[:, low], nhalo.at[1], s_q.at[2], r_q.at[3])
    near_right = to_right(nsum.at[:, high], nhalo.at[0], s_q.at[3], r_q.at[2])
    crossing = []
    for a in range(2):
        rows = pl.ds(a * RL * R, RL * R)
        for h in range(halves):
            for cp in far_parts[a][h]:
                cp.wait_recv()
            add_parts(h, far_case, a, rfar, fsum)
            crossing.append(push(remote(
                fsum.at[h, rows], rz.at[h, rows], s_pz.at[h, a], r_pz.at[h, a], z_dev(zl_n)
            )))
        send_sides([far_left] if a == 0 else [], [] if a == 0 else [far_right])
    for a in range(2):
        for h in range(halves):
            for cp in near_parts[a][h]:
                cp.wait_recv()
            add_parts(h, c, a, rnear, nsum)
    send_sides([near_left], [near_right])
    for cp in crossing:
        cp.wait_recv()

    @pl.when(has_left)
    def _():
        near_right.wait_recv()
        far_right.wait_recv()

    @pl.when(has_right)
    def _():
        near_left.wait_recv()
        far_left.wait_recv()

    def wide(first, second, rows):
        return jnp.concatenate([first[h, rows, :] + second[h, rows, :] for h in range(halves)], axis=1)

    every = slice(0, R)
    qs = [wide(nhalo.at[0], rhalo.at[0], every)]
    qs += [wide(nsum, rz, slice(l * R, (l + 1) * R)) for l in range(R)]
    qs += [wide(nhalo.at[1], rhalo.at[1], every)]
    abs_vec = zero
    for l in range(R):
        v = qs[l + 1]
        before = jnp.where(y_first, wide(nsum, rz, slice(8 * R + l, 8 * R + l + 1)), pltpu.roll(v, 1, 0))
        after = jnp.where(y_last, wide(nsum, rz, slice(9 * R + l, 9 * R + l + 1)), pltpu.roll(v, R - 1, 0))
        value = (
            2.0 * v + qs[l] + qs[l + 2] + before + after
            + jnp.where(z_first, 0.0, z_prev(v)) + jnp.where(z_last, 0.0, z_next(v))
        )
        sens[l] = value
        abs_vec = abs_vec + jnp.abs(value)

    pl.semaphore_wait(round_sem.at[1], len(met))
    lane1 = lax.broadcasted_iota(jnp.int32, (1, 128), 1)
    now = jnp.where(lane1 == 8, jnp.sum(abs_vec, axis=(0, 1), keepdims=True), jnp.where(lane1 == c, obj_part, 0.0))
    def ring(d, n):
        return min(d, n - d)

    plane_order = sorted(range(1, YD * XC), key=lambda k: -ring(k // XC, YD) - ring(k % XC, XC) / 2)
    z_order = sorted(range(1, z_n), key=lambda k: -ring(k, z_n))
    for i, (buf, ssem, rsem, order, dev) in enumerate(
        [(arx, s_ax, r_ax, plane_order, plane_dev), (arz, s_az, r_az, z_order, z_dev)]
    ):
        msg[i] = now
        before = list(sends)
        copies = [
            push(remote(msg.at[i], buf.at[k - 1], ssem.at[k - 1], rsem.at[k - 1], dev(k))) for k in order
        ]
        if i == 1:
            sends[:] = before
            drain()
            sends[:] = [(None, cp) for cp in copies]
        for cp in copies:
            cp.wait_recv()
        now = now + jnp.sum(buf[...], axis=0)

    total_abs = jnp.sum(jnp.where(lane1 == 8, now, 0.0), axis=(0, 1), keepdims=True)
    scale = 1.0 / (total_abs / (grid_rows * R * R * width) + 1e-06)
    obj_out[...] = jnp.zeros_like(obj_out) + jnp.sum(jnp.where(lane1 == c, now, 0.0), axis=(0, 1), keepdims=True)
    for l in range(R):
        sens_out[l] = sens[l] * scale

    drain()


def body(density, heat_power, laser_mask, sink_mask):
    tiles = lax.axis_size("tile")
    rows, grid_y, width = sink_mask.shape
    halves = width // 128
    pieces = halves * R // HL
    f32 = jnp.float32
    z_n = ZH * (tiles // XC)

    def vm(*shape):
        return pltpu.VMEM(shape, f32)

    def dma(*shape):
        return pltpu.SemaphoreType.DMA(shape)

    scratch = [
        vm(EXT, halves, grid_y, 128),
        vm(pieces, HL, R, 128),
        vm(rows, halves, grid_y, 128),
        pltpu.VMEM((rows, halves, grid_y, 128), jnp.int32),
        pltpu.VMEM((EXT, halves, grid_y, 128), jnp.int32),
        vm(EXT, halves, grid_y, 128),
        vm(EXT, halves, grid_y, 128),
        vm(2, EXT, halves, grid_y, 128),
    ]
    for count in (YD, YD + 1):
        scratch += [vm(EXT, count, R, width)] * 7 + [vm(2, EXT, count, R, width)] * (SWEEPS - 1)
    scratch += [
        vm(halves, 8 * 10 * R, 128),
        vm(YD - 1, halves, 10 * R, 128),
        vm(YD - 1, halves, 10 * R, 128),
        vm(halves, 10 * R, 128),
        vm(halves, 10 * R, 128),
        vm(halves, 10 * R, 128),
        vm(2, halves, R, 128),
        vm(2, halves, R, 128),
        vm(R, R, width),
        vm(2, 1, 128),
        vm(YD * XC - 1, 1, 128),
        vm(z_n - 1, 1, 128),
        dma(halves, 4),
        pltpu.SemaphoreType.REGULAR((2,)),
        dma(pieces), dma(pieces),
        dma(YD - 1, pieces), dma(YD - 1, pieces),
        dma(pieces), dma(pieces),
        dma(YD - 1, pieces), dma(YD - 1, pieces),
        dma(2, YD), dma(2, YD),
        dma(2, YD, pieces), dma(2, YD, pieces),
        dma(4), dma(4),
        dma(2, YD - 1, halves, 2), dma(2, YD - 1, halves, 2),
        dma(halves, 2), dma(halves, 2),
        dma(4), dma(4),
        dma(YD * XC - 1), dma(YD * XC - 1),
        dma(z_n - 1), dma(z_n - 1),
    ]
    any_spec = pl.BlockSpec(memory_space=pl.ANY)
    vmem_spec = pl.BlockSpec(memory_space=pltpu.VMEM)
    sensitivity, objective = pl.pallas_call(
        functools.partial(kernel, tiles),
        out_shape=(
            jax.ShapeDtypeStruct(density.shape, f32),
            jax.ShapeDtypeStruct((1, 128), f32),
        ),
        in_specs=[any_spec] * 4,
        out_specs=(vmem_spec, vmem_spec),
        scratch_shapes=scratch,
        compiler_params=pltpu.CompilerParams(
            collective_id=0, has_side_effects=True, vmem_limit_bytes=56150000
        ),
    )(density, heat_power, laser_mask, sink_mask)
    return sensitivity, objective[0, :1]


def solution(mesh):
    return jax.shard_map(
        body,
        mesh=mesh,
        in_specs=(
            P("tile", "case", None),
            P("case", "tile", None, None),
            P("case", "tile", None, None),
            P("tile", None, None),
        ),
        out_specs=(P("tile", "case", None), P("case")),
        check_vma=False,
    )
```

```python
import functools

import jax
import jax.numpy as jnp
from jax import lax
from jax.experimental import pallas as pl
from jax.experimental.pallas import tpu as pltpu
from jax.sharding import PartitionSpec as P

SWEEPS = 6
heat_loss = 0.02
low_cond = 0.01
eig_low = 0.08
eig_high = 2.0

MESH = pl.DeviceIdType.MESH
UNROLL = (6, 4, 7, 6, 5)
YD = 4
ZH = 2
XC = 8
R = 8
HL = 4
RL = 5
EXT = 3 * R


def horner_coefficients():
    centre = 0.5 * (eig_high + eig_low)
    half = 0.5 * (eig_high - eig_low)
    ratio = centre / half
    weight = 1.0 / ratio
    x = [1.0 / centre] + [0.0] * (SWEEPS - 1)
    s = list(x)
    for _ in range(1, SWEEPS):
        nxt = 1.0 / (2.0 * ratio - weight)
        r = [-a for a in x]
        r[0] += 1.0
        for k in range(1, SWEEPS):
            r[k] += x[k - 1]
        s = [nxt * weight * a + 2.0 * nxt / half * b for a, b in zip(s, r)]
        x = [a + b for a, b in zip(x, s)]
        weight = nxt
    return x


COEF = horner_coefficients()
LEAD = COEF[-1]


def kernel(
    tiles,
    dens_in, heat_in, laser_in, sink_in,
    sens_out, obj_out,
    dens, relay, heat, laser, sink, src, wgt, fin, *rest,
):
    near_set, far_set, rest = rest[:12], rest[12:24], rest[24:]
    (
        part, rfar, rnear, fsum, rz, nsum, nhalo, rhalo, sens, msg, arx, arz, lsem, round_sem, s_zr, r_zr, s_y, r_y, s_z, r_z, s_yf, r_yf, s_t, r_t, s_tf, r_tf, s_h, r_h, s_p, r_p, s_pz, r_pz, s_q, r_q, s_ax, r_ax, s_az, r_az,
    ) = rest
    zl_n = tiles // XC
    z_n = ZH * zl_n
    c = lax.axis_index("case")
    t = lax.axis_index("tile")
    zh = c // YD
    yy = c % YD
    zl = t // XC
    xc = t % XC
    z = zh * zl_n + zl
    has_left = t > 0
    has_right = t < tiles - 1
    halves = dens.shape[1]
    width = 128 * halves

    def y_case(d):
        return zh * YD + (yy + d) % YD

    def z_dev(d):
        zz = (z + d) % z_n
        return {"case": (zz // zl_n) * YD + yy, "tile": (zz % zl_n) * XC + xc}

    def x_tile(d):
        return zl * XC + (xc + d) % XC

    def plane_dev(k):
        return {"case": y_case(k // XC), "tile": x_tile(k % XC)}

    barrier = pltpu.get_barrier_semaphore()

    def greet(dev):
        pl.semaphore_signal(barrier, inc=1, device_id=dev, device_id_type=MESH)

    met = [z_dev(d) for d in (1, 2, 4, z_n - 1, z_n - 2, z_n - 4)]
    met += [{"case": y_case(d), "tile": t} for d in range(1, YD)]
    met += [{"case": c, "tile": x_tile(d)} for d in range(1, XC)]
    for dev in met:
        greet(dev)

    @pl.when(has_left)
    def _():
        greet({"case": c, "tile": t - 1})

    @pl.when(has_right)
    def _():
        greet({"case": c, "tile": t + 1})

    slab = pl.ds(pl.multiple_of(c * R, R), R)
    loads = []
    for h in range(halves):
        lanes = pl.ds(h * 128, 128)
        loads.append([
            pltpu.make_async_copy(dens_in.at[:, :, lanes], dens.at[pl.ds(R, R), h, slab, :], lsem.at[h, 0]),
            pltpu.make_async_copy(heat_in.at[0, :, :, lanes], heat.at[:, h], lsem.at[h, 1]),
            pltpu.make_async_copy(laser_in.at[0, :, :, lanes], laser.at[:, h], lsem.at[h, 2]),
            pltpu.make_async_copy(sink_in.at[:, :, lanes], sink.at[pl.ds(R, R), h], lsem.at[h, 3]),
        ])
    for k in range(4):
        for h in range(halves):
            loads[h][k].start()

    @pl.when(t == 0)
    def _():
        dens[0:R] = jnp.zeros((R,) + dens.shape[1:], jnp.float32)
        src[2:R] = jnp.zeros((R - 2,) + src.shape[1:], jnp.float32)
        sink[2:R] = jnp.zeros((R - 2,) + sink.shape[1:], jnp.int32)
        nhalo[0] = jnp.zeros(nhalo.shape[1:], jnp.float32)
        rhalo[0] = jnp.zeros(rhalo.shape[1:], jnp.float32)

    @pl.when(t == tiles - 1)
    def _():
        dens[2 * R:] = jnp.zeros((R,) + dens.shape[1:], jnp.float32)
        src[2 * R:3 * R - 2] = jnp.zeros((R - 2,) + src.shape[1:], jnp.float32)
        sink[2 * R:3 * R - 2] = jnp.zeros((R - 2,) + sink.shape[1:], jnp.int32)
        nhalo[1] = jnp.zeros(nhalo.shape[1:], jnp.float32)
        rhalo[1] = jnp.zeros(rhalo.shape[1:], jnp.float32)

    def make_source(l, carry):
        for j in range(R):
            for h in range(halves):
                rows = pl.ds(j * R, R)
                src[l + R, h, rows, :] = heat[l, h, rows, :] * laser[l, h, rows, :].astype(jnp.float32)
        return carry

    pl.semaphore_wait(
        barrier, len(met) + has_left.astype(jnp.int32) + has_right.astype(jnp.int32)
    )

    sends = []

    def drain():
        for guard, group in ((None, []), (has_left, []), (has_right, [])):
            group = [cp for g, cp in sends if g is guard]
            if not group:
                continue

            def wait_all(group=group):
                for cp in group:
                    cp.wait_send()

            if guard is None:
                wait_all()
            else:
                pl.when(guard)(wait_all)

    def push(cp):
        cp.start()
        sends.append((None, cp))
        return cp

    def remote(a, b, ssem, rsem, dev):
        return pltpu.make_async_remote_copy(
            src_ref=a, dst_ref=b, send_sem=ssem, recv_sem=rsem, device_id=dev, device_id_type=MESH
        )

    def to_left(a, b, ssem, rsem):
        return remote(a, b, ssem, rsem, {"case": c, "tile": jnp.maximum(t - 1, 0)})

    def to_right(a, b, ssem, rsem):
        return remote(a, b, ssem, rsem, {"case": c, "tile": jnp.minimum(t + 1, tiles - 1)})

    def piece(base, k, rows):
        return dens.at[pl.ds(base + (k // halves) * HL, HL), k % halves, rows, :]

    def piece_in(k):
        return dens_in.at[pl.ds((k // halves) * HL, HL), :, pl.ds((k % halves) * 128, 128)]

    pieces = halves * R // HL
    quarter = z_n // 4
    column = xc // 2
    via = []
    for k in range(pieces):
        way = quarter if k < pieces // 2 else z_n - quarter
        if k < pieces - 1:
            way = jnp.where(column == 0, quarter, way)
        if k > 0:
            way = jnp.where(column == XC // 2 - 1, z_n - quarter, way)
        via.append(way)
    for k in range(pieces):
        push(remote(piece_in(k), relay.at[k], s_zr.at[k], r_zr.at[k], z_dev(via[k])))
    y_copies = []
    for d in range(1, YD):
        to = {"case": y_case(d), "tile": t}
        y_copies.append([
            push(remote(piece_in(k), piece(R, k, slab), s_y.at[d - 1, k], r_y.at[d - 1, k], to))
            for k in range(pieces)
        ])

    for dev in met:
        pl.semaphore_signal(round_sem.at[0], inc=1, device_id=dev, device_id_type=MESH)
    for h in range(halves):
        loads[h][3].wait()

    halo_left = [
        to_left(src.at[pl.ds(R, R - 2)], src.at[pl.ds(2 * R, R - 2)], s_h.at[0], r_h.at[1]),
        to_left(sink.at[pl.ds(R, R - 2)], sink.at[pl.ds(2 * R, R - 2)], s_h.at[1], r_h.at[3]),
    ]
    halo_right = [
        to_right(src.at[pl.ds(R + 2, R - 2)], src.at[pl.ds(2, R - 2)], s_h.at[2], r_h.at[0]),
        to_right(sink.at[pl.ds(R + 2, R - 2)], sink.at[pl.ds(2, R - 2)], s_h.at[3], r_h.at[2]),
    ]

    def send_sides(left, right):
        @pl.when(has_left)
        def _():
            for cp in left:
                cp.start()

        @pl.when(has_right)
        def _():
            for cp in right:
                cp.start()

        sends.extend((has_left, cp) for cp in left)
        sends.extend((has_right, cp) for cp in right)

    send_sides(halo_left[1:], halo_right[1:])
    for k in range(3):
        for h in range(halves):
            loads[h][k].wait()
    lax.fori_loop(0, R, make_source, 0)

    def slab_of(case):
        return pl.ds(pl.multiple_of(case * R, R), R)

    tile_copies = []

    def forward(case, order):
        rows = slab_of(case)
        here = dens.at[pl.ds(R, R), :, rows, :]
        left = to_left(here, dens.at[pl.ds(2 * R, R), :, rows, :], s_t.at[0, order], r_t.at[1, order])
        right = to_right(here, dens.at[pl.ds(0, R), :, rows, :], s_t.at[1, order], r_t.at[0, order])
        send_sides([left], [right])
        tile_copies.append((left, right))

    def forward_piece(case, order, k):
        rows = slab_of(case)
        here = piece(R, k, rows)
        left = to_left(here, piece(2 * R, k, rows), s_tf.at[0, order, k], r_tf.at[1, order, k])
        right = to_right(here, piece(0, k, rows), s_tf.at[1, order, k], r_tf.at[0, order, k])
        send_sides([left], [right])
        tile_copies.append((left, right))

    forward(c, 0)
    for d in range(1, YD):
        for cp in y_copies[d - 1]:
            cp.wait_recv()
        forward(zh * YD + (yy + YD - d) % YD, d)

    send_sides(halo_left[:1], halo_right[:1])

    z_copies = []
    for k in range(pieces):
        into = relay.at[k]
        remote(into, into, s_zr.at[k], r_zr.at[k], z_dev(via[k])).wait_recv()
        origin = z_dev(z_n - via[k])["case"]
        z_copies.append(
            push(remote(into, piece(R, k, slab_of(origin)), s_z.at[k], r_z.at[k], z_dev(via[k])))
        )
    pl.semaphore_wait(round_sem.at[0], len(met))
    for dev in met:
        pl.semaphore_signal(round_sem.at[1], inc=1, device_id=dev, device_id_type=MESH)

    far = (1 - zh) * YD
    far_case = far + yy
    yf_copies = []

    def cross(k):
        z_copies[k].wait_recv()
        here = piece(R, k, slab_of(far_case))
        yf_copies.append({
            d: push(remote(here, here, s_yf.at[d - 1, k], r_yf.at[d - 1, k], {"case": y_case(d), "tile": t}))
            for d in (2, 1, 3)
        })
        forward_piece(far_case, 0, k)

    def spread(k):
        for d in (1, 3, 2):
            yf_copies[k][d].wait_recv()
            forward_piece(far + (yy + YD - d) % YD, d, k)

    for k in range(pieces):
        cross(k)

    def wait_sides(left, right):
        @pl.when(has_left)
        def _():
            for cp in right:
                cp.wait_recv()

        @pl.when(has_right)
        def _():
            for cp in left:
                cp.wait_recv()

    def wait_tiles(pairs):
        wait_sides([left for left, _ in pairs], [right for _, right in pairs])

    lane = lax.broadcasted_iota(jnp.int32, (R, width), 1)
    sub = lax.broadcasted_iota(jnp.int32, (R, width), 0)
    z_first = lane == 0
    z_last = lane == width - 1
    y_first = sub == 0
    y_last = sub == R - 1
    zero = jnp.zeros((R, width), jnp.float32)
    one = jnp.ones((R, width), jnp.float32)
    grid_rows = tiles * R

    def z_prev(v):
        return pltpu.roll(v, 1, 1)

    def z_next(v):
        return pltpu.roll(v, width - 1, 1)

    lane_h = lax.broadcasted_iota(jnp.int32, (R, 128), 1)

    def z_from_prev(v):
        turned = [pltpu.roll(v[:, h * 128:(h + 1) * 128], 1, 1) for h in range(halves)]
        out = turned[:1] + [jnp.where(lane_h == 0, turned[h - 1], turned[h]) for h in range(1, halves)]
        return jnp.concatenate(out, axis=1)

    def z_from_next(v):
        turned = [pltpu.roll(v[:, h * 128:(h + 1) * 128], 127, 1) for h in range(halves)]
        out = [jnp.where(lane_h == 127, turned[h + 1], turned[h]) for h in range(halves - 1)] + turned[-1:]
        return jnp.concatenate(out, axis=1)

    def flag(cond_):
        return cond_.astype(jnp.float32)

    def inside(g):
        return (g >= 0) & (g < grid_rows)

    class Rows:
        def __init__(self, base, count, refs, near=None):
            self.base, self.count, self.near = base, count, near
            self.cond, *self.ks = refs[:7]
            self.ys = refs[7:]
            self.low = 0.0 if near is None else flag(zh == 0)
            self.high = 0.0 if near is None else flag(zh == 1)

        def rows(self, j):
            return pl.ds(self.base + j, R, stride=self.count)

        def load(self, ref, e, j):
            return jnp.concatenate([ref[e, h, self.rows(j), :] for h in range(halves)], axis=1)

        def store(self, ref, e, j, value):
            for h in range(halves):
                ref[e, h, self.rows(j), :] = value[:, h * 128:(h + 1) * 128]

        def around(self, planes, outer=None):
            first = pltpu.roll(planes[-1], 1, 0)
            last = pltpu.roll(planes[0], R - 1, 0)
            if outer is not None:
                first = jnp.where(y_first, outer[0], first)
                last = jnp.where(y_last, outer[1], last)
            return [first] + planes[:-1], planes[1:] + [last]

        def outer(self, get):
            if self.near is None:
                return None
            return get(self.near, YD - 1)[5:6], get(self.near, 0)[2:3]

    def physical_step(e, part_):
        g = t * R - R + e
        nx = 2.0 + flag(g > 0) + flag(g < grid_rows - 1)
        nyz = nx + jnp.where(z_first | z_last, 1.0, 2.0)
        planes = [part_.load(dens, e, j) for j in range(part_.count)]
        outside = None
        if part_.near is not None:
            outside = [
                jnp.concatenate([dens[e, h, y:y + 1, :] for h in range(halves)], axis=1)
                for y in (3 * R - 1, 5 * R)
            ]
        befores, afters = part_.around(planes, outside)
        for j in range(part_.count):
            v, before, after = planes[j], befores[j], afters[j]
            ny = 2.0
            if j == 0:
                has = jnp.where(y_first, part_.low, 1.0)
                before = before * has
                ny = 1.0 + has
            if j == part_.count - 1:
                has = jnp.where(y_last, part_.high, 1.0)
                after = after * has
                ny = 1.0 + has
            total = (
                2.0 * v + part_.load(dens, e - 1, j) + part_.load(dens, e + 1, j) + before + after
                + jnp.where(z_first, 0.0, z_prev(v)) + jnp.where(z_last, 0.0, z_next(v))
            )
            inv = 1.0 / (nyz + ny)
            phys = total * inv
            sq = phys * phys
            part_.cond[e, j] = low_cond + (1.0 - low_cond) * (sq * phys)
            part_.store(wgt, e, j, (-1.5 * (1.0 - low_cond) * LEAD * LEAD) * sq * inv)

    def face_step(e, part_):
        g = t * R - R + e
        vm = 0.5 * flag(inside(g - 1) & inside(g))
        vp = 0.5 * flag(inside(g) & inside(g + 1))
        cond = part_.cond
        planes = [cond[e, j] for j in range(part_.count)]
        befores, afters = part_.around(planes, part_.outer(lambda near, j: near.cond[e, j]))
        for j in range(part_.count):
            v = planes[j]
            f_xm = vm * (cond[e - 1, j] + v)
            f_xp = vp * (cond[e + 1, j] + v)
            f_ym = 0.5 * (befores[j] + v)
            f_yp = 0.5 * (afters[j] + v)
            if j == 0:
                f_ym = f_ym * jnp.where(y_first, part_.low, 1.0)
            if j == part_.count - 1:
                f_yp = f_yp * jnp.where(y_last, part_.high, 1.0)
            f_zm = jnp.where(z_first, 0.0, 0.5 * (z_prev(v) + v))
            f_zp = jnp.where(z_last, 0.0, 0.5 * (z_next(v) + v))
            diag = heat_loss + f_xm + f_xp + f_ym + f_yp + f_zm + f_zp
            free = jnp.where(part_.load(sink, e, j) == 0, 1.0, 0.0)
            scale = free / diag
            for ref, face in zip(part_.ks, (f_xm, f_xp, f_ym, f_yp, f_zm, f_zp)):
                ref[e, j] = scale * face
            source = part_.load(src, e, j)
            part_.ys[0][0, e, j] = scale * source
            part_.ys[0][1, e, j] = jnp.where(source > 0.0, scale, 0.0)

    def sweep_step(n, e, part_):
        ratio = COEF[SWEEPS - 2 - n] / LEAD
        bias, y_in = part_.ys[0], part_.ys[n]
        for f in range(2):
            planes = [y_in[f, e, j] for j in range(part_.count)]
            befores, afters = part_.around(planes, part_.outer(lambda near, j: near.ys[n][f, e, j]))
            for j in range(part_.count):
                ks = [ref[e, j] for ref in part_.ks]
                acc = ratio * bias[f, e, j]
                acc = acc + ks[0] * y_in[f, e - 1, j]
                acc = acc + ks[1] * y_in[f, e + 1, j]
                acc = acc + ks[2] * befores[j]
                acc = acc + ks[3] * afters[j]
                acc = acc + ks[4] * z_from_prev(planes[j])
                acc = acc + ks[5] * z_from_next(planes[j])
                if n == SWEEPS - 2:
                    part_.store(fin.at[f], e, j, acc)
                else:
                    part_.ys[n + 1][f, e, j] = acc

    def over_layers(step, low, high, unroll=1):
        def body(e, carry):
            step(e)
            return carry

        lax.fori_loop(low, high, body, 0, unroll=unroll)

    def set_up_rows(part_, low=1, high=EXT - 1):
        over_layers(lambda e: physical_step(e, part_), low, high, 2)

    def face_rows(part_, low=2, high=EXT - 2):
        over_layers(lambda e: face_step(e, part_), low, high, 2)

    def solve_rows(part_):
        for n in range(SWEEPS - 1):
            over_layers(lambda e, n=n: sweep_step(n, e, part_), 3 + n, EXT - 3 - n, UNROLL[n])

    near = Rows(zh * (YD * R), YD, near_set)
    beyond = Rows((1 - zh) * (3 * R), YD + 1, far_set, near)
    wait_tiles(tile_copies[:YD])
    set_up_rows(near)
    wait_sides(halo_left, halo_right)
    face_rows(near)
    for k in range(pieces):
        spread(k)
    solve_rows(near)
    set_up_rows(beyond, R + 1, 2 * R - 1)
    face_rows(beyond, R + 2, 2 * R - 2)
    wait_tiles(tile_copies[YD:])
    set_up_rows(beyond, 1, R + 1)
    set_up_rows(beyond, 2 * R - 1, EXT - 1)
    face_rows(beyond, 2, R + 2)
    face_rows(beyond, 2 * R - 2, EXT - 2)
    solve_rows(beyond)

    def row_load(ref, e, k):
        return jnp.concatenate([ref[e, h, k * R:(k + 1) * R, :] for h in range(halves)], axis=1)

    def slab_store(row, value):
        for h in range(halves):
            part[h, pl.ds(row, value.shape[0]), :] = value[:, h * 128:(h + 1) * 128]

    def product_step(e, total):
        g = t * R - R + e
        l = e - R
        vm = flag(inside(g - 1))
        vp = flag(inside(g + 1))
        ps = [row_load(fin.at[0], e, k) for k in range(R)]
        qs = [row_load(fin.at[1], e, k) for k in range(R)]
        down = []
        for k in range(R):
            up = min(k + 1, R - 1)
            pn = jnp.where(y_last, pltpu.roll(ps[up], R - 1, 0), pltpu.roll(ps[k], R - 1, 0))
            qn = jnp.where(y_last, pltpu.roll(qs[up], R - 1, 0), pltpu.roll(qs[k], R - 1, 0))
            face = (ps[k] - pn) * (qs[k] - qn)
            if k == R - 1:
                face = jnp.where(y_last, 0.0, face)
            down.append((face, pltpu.roll(face, 1, 0)))
        for k in range(R):
            p, q = ps[k], qs[k]
            acc = vm * ((p - row_load(fin.at[0], e - 1, k)) * (q - row_load(fin.at[1], e - 1, k)))
            acc = acc + vp * ((p - row_load(fin.at[0], e + 1, k)) * (q - row_load(fin.at[1], e + 1, k)))
            above = down[k - 1][1] if k > 0 else 0.0
            acc = acc + down[k][0] + jnp.where(y_first, above, down[k][1])
            face = jnp.where(z_last, 0.0, (p - z_next(p)) * (q - z_next(q)))
            acc = (acc + face + z_prev(face)) * row_load(wgt, e, k)
            slab_store(pl.multiple_of(k * 10 * R + l * R, R), acc)
            if k < R - 1:
                slab_store((k + 1) * 10 * R + 8 * R + l, acc[R - 1:])
            if k > 0:
                slab_store((k - 1) * 10 * R + 9 * R + l, acc[:1])
            total = total + jnp.where(row_load(src, e, k) > 0.0, p, 0.0)
        return total

    for h in range(halves):
        part[h, 8 * R:9 * R, :] = jnp.zeros((R, 128), jnp.float32)
        part[h, 7 * 10 * R + 9 * R:7 * 10 * R + 10 * R, :] = jnp.zeros((R, 128), jnp.float32)

    obj_vec = lax.fori_loop(R, R + RL, product_step, zero)

    def part_rows(case, a):
        return pl.ds(pl.multiple_of(case * (10 * R) + a * RL * R, R), RL * R)

    def y_parts(side, dest_base, a, buf):
        rows = pl.ds(a * RL * R, RL * R)
        return [
            [
                push(remote(
                    part.at[h, part_rows(dest_base + (yy + d) % YD, a)], buf.at[d - 1, h, rows],
                    s_p.at[side, d - 1, h, a], r_p.at[side, d - 1, h, a], {"case": y_case(d), "tile": t},
                ))
                for d in range(1, YD)
            ]
            for h in range(halves)
        ]

    def add_parts(h, case, a, buf, out):
        base = case * (10 * R)

        def step(i, carry):
            rows = pl.ds(pl.multiple_of(i * R, R), R)
            mine = part[h, pl.ds(pl.multiple_of(base + i * R, R), R), :]
            out[h, rows, :] = (mine + buf[0, h, rows, :]) + (buf[1, h, rows, :] + buf[2, h, rows, :])
            return carry

        lax.fori_loop(a * RL, (a + 1) * RL, step, 0, unroll=RL)

    far_parts = [y_parts(0, far, 0, rfar)]
    obj_vec = lax.fori_loop(R + RL, 2 * R, product_step, obj_vec)
    far_parts.append(y_parts(0, far, 1, rfar))
    near_parts = [y_parts(1, zh * YD, a, rnear) for a in range(2)]
    obj_part = LEAD * jnp.sum(obj_vec, axis=(0, 1), keepdims=True)

    low = pl.ds(0, R)
    high = pl.ds((R - 1) * R, R)
    left_case = {"case": far_case, "tile": jnp.maximum(t - 1, 0)}
    right_case = {"case": far_case, "tile": jnp.minimum(t + 1, tiles - 1)}
    far_left = remote(fsum.at[:, low], rhalo.at[1], s_q.at[0], r_q.at[1], left_case)
    far_right = remote(fsum.at[:, high], rhalo.at[0], s_q.at[1], r_q.at[0], right_case)
    near_left = to_left(nsum.at[:, low], nhalo.at[1], s_q.at[2], r_q.at[3])
    near_right = to_right(nsum.at[:, high], nhalo.at[0], s_q.at[3], r_q.at[2])
    crossing = []
    for a in range(2):
        rows = pl.ds(a * RL * R, RL * R)
        for h in range(halves):
            for cp in far_parts[a][h]:
                cp.wait_recv()
            add_parts(h, far_case, a, rfar, fsum)
            crossing.append(push(remote(
                fsum.at[h, rows], rz.at[h, rows], s_pz.at[h, a], r_pz.at[h, a], z_dev(zl_n)
            )))
        send_sides([far_left] if a == 0 else [], [] if a == 0 else [far_right])
    for a in range(2):
        for h in range(halves):
            for cp in near_parts[a][h]:
                cp.wait_recv()
            add_parts(h, c, a, rnear, nsum)
    send_sides([near_left], [near_right])
    for cp in crossing:
        cp.wait_recv()

    @pl.when(has_left)
    def _():
        near_right.wait_recv()
        far_right.wait_recv()

    @pl.when(has_right)
    def _():
        near_left.wait_recv()
        far_left.wait_recv()

    def wide(first, second, rows):
        return jnp.concatenate([first[h, rows, :] + second[h, rows, :] for h in range(halves)], axis=1)

    every = slice(0, R)
    qs = [wide(nhalo.at[0], rhalo.at[0], every)]
    qs += [wide(nsum, rz, slice(l * R, (l + 1) * R)) for l in range(R)]
    qs += [wide(nhalo.at[1], rhalo.at[1], every)]
    abs_vec = zero
    for l in range(R):
        v = qs[l + 1]
        before = jnp.where(y_first, wide(nsum, rz, slice(8 * R + l, 8 * R + l + 1)), pltpu.roll(v, 1, 0))
        after = jnp.where(y_last, wide(nsum, rz, slice(9 * R + l, 9 * R + l + 1)), pltpu.roll(v, R - 1, 0))
        value = (
            2.0 * v + qs[l] + qs[l + 2] + before + after
            + jnp.where(z_first, 0.0, z_prev(v)) + jnp.where(z_last, 0.0, z_next(v))
        )
        sens[l] = value
        abs_vec = abs_vec + jnp.abs(value)

    pl.semaphore_wait(round_sem.at[1], len(met))
    lane1 = lax.broadcasted_iota(jnp.int32, (1, 128), 1)
    now = jnp.where(lane1 == 8, jnp.sum(abs_vec, axis=(0, 1), keepdims=True), jnp.where(lane1 == c, obj_part, 0.0))
    def ring(d, n):
        return min(d, n - d)

    plane_order = sorted(range(1, YD * XC), key=lambda k: -ring(k // XC, YD) - ring(k % XC, XC) / 2)
    z_order = sorted(range(1, z_n), key=lambda k: -ring(k, z_n))
    for i, (buf, ssem, rsem, order, dev) in enumerate(
        [(arx, s_ax, r_ax, plane_order, plane_dev), (arz, s_az, r_az, z_order, z_dev)]
    ):
        msg[i] = now
        before = list(sends)
        copies = [
            push(remote(msg.at[i], buf.at[k - 1], ssem.at[k - 1], rsem.at[k - 1], dev(k))) for k in order
        ]
        if i == 1:
            sends[:] = before
            drain()
            sends[:] = [(None, cp) for cp in copies]
        for cp in copies:
            cp.wait_recv()
        now = now + jnp.sum(buf[...], axis=0)

    total_abs = jnp.sum(jnp.where(lane1 == 8, now, 0.0), axis=(0, 1), keepdims=True)
    scale = 1.0 / (total_abs / (grid_rows * R * R * width) + 1e-06)
    obj_out[...] = jnp.zeros_like(obj_out) + jnp.sum(jnp.where(lane1 == c, now, 0.0), axis=(0, 1), keepdims=True)
    for l in range(R):
        sens_out[l] = sens[l] * scale

    drain()


def body(density, heat_power, laser_mask, sink_mask):
    tiles = lax.axis_size("tile")
    rows, grid_y, width = sink_mask.shape
    halves = width // 128
    pieces = halves * R // HL
    f32 = jnp.float32
    z_n = ZH * (tiles // XC)

    def vm(*shape):
        return pltpu.VMEM(shape, f32)

    def dma(*shape):
        return pltpu.SemaphoreType.DMA(shape)

    scratch = [
        vm(EXT, halves, grid_y, 128),
        vm(pieces, HL, R, 128),
        vm(rows, halves, grid_y, 128),
        pltpu.VMEM((rows, halves, grid_y, 128), jnp.int32),
        pltpu.VMEM((EXT, halves, grid_y, 128), jnp.int32),
        vm(EXT, halves, grid_y, 128),
        vm(EXT, halves, grid_y, 128),
        vm(2, EXT, halves, grid_y, 128),
    ]
    for count in (YD, YD + 1):
        scratch += [vm(EXT, count, R, width)] * 7 + [vm(2, EXT, count, R, width)] * (SWEEPS - 1)
    scratch += [
        vm(halves, 8 * 10 * R, 128),
        vm(YD - 1, halves, 10 * R, 128),
        vm(YD - 1, halves, 10 * R, 128),
        vm(halves, 10 * R, 128),
        vm(halves, 10 * R, 128),
        vm(halves, 10 * R, 128),
        vm(2, halves, R, 128),
        vm(2, halves, R, 128),
        vm(R, R, width),
        vm(2, 1, 128),
        vm(YD * XC - 1, 1, 128),
        vm(z_n - 1, 1, 128),
        dma(halves, 4),
        pltpu.SemaphoreType.REGULAR((2,)),
        dma(pieces), dma(pieces),
        dma(YD - 1, pieces), dma(YD - 1, pieces),
        dma(pieces), dma(pieces),
        dma(YD - 1, pieces), dma(YD - 1, pieces),
        dma(2, YD), dma(2, YD),
        dma(2, YD, pieces), dma(2, YD, pieces),
        dma(4), dma(4),
        dma(2, YD - 1, halves, 2), dma(2, YD - 1, halves, 2),
        dma(halves, 2), dma(halves, 2),
        dma(4), dma(4),
        dma(YD * XC - 1), dma(YD * XC - 1),
        dma(z_n - 1), dma(z_n - 1),
    ]
    any_spec = pl.BlockSpec(memory_space=pl.ANY)
    vmem_spec = pl.BlockSpec(memory_space=pltpu.VMEM)
    sensitivity, objective = pl.pallas_call(
        functools.partial(kernel, tiles),
        out_shape=(
            jax.ShapeDtypeStruct(density.shape, f32),
            jax.ShapeDtypeStruct((1, 128), f32),
        ),
        in_specs=[any_spec] * 4,
        out_specs=(vmem_spec, vmem_spec),
        scratch_shapes=scratch,
        compiler_params=pltpu.CompilerParams(
            collective_id=0, has_side_effects=True, vmem_limit_bytes=56460000
        ),
    )(density, heat_power, laser_mask, sink_mask)
    return sensitivity, objective[0, :1]


def solution(mesh):
    return jax.shard_map(
        body,
        mesh=mesh,
        in_specs=(
            P("tile", "case", None),
            P("case", "tile", None, None),
            P("case", "tile", None, None),
            P("tile", None, None),
        ),
        out_specs=(P("tile", "case", None), P("case")),
        check_vma=False,
    )
```

```python
import functools

import jax
import jax.numpy as jnp
from jax import lax
from jax.experimental import pallas as pl
from jax.experimental.pallas import tpu as pltpu
from jax.sharding import PartitionSpec as P

SWEEPS = 6
heat_loss = 0.02
low_cond = 0.01
eig_low = 0.08
eig_high = 2.0

MESH = pl.DeviceIdType.MESH
UNROLL = (6, 4, 7, 6, 5)
YD = 4
ZH = 2
XC = 8
R = 8
HL = 4
RL = 5
EXT = 3 * R


def horner_coefficients():
    centre = 0.5 * (eig_high + eig_low)
    half = 0.5 * (eig_high - eig_low)
    ratio = centre / half
    weight = 1.0 / ratio
    x = [1.0 / centre] + [0.0] * (SWEEPS - 1)
    s = list(x)
    for _ in range(1, SWEEPS):
        nxt = 1.0 / (2.0 * ratio - weight)
        r = [-a for a in x]
        r[0] += 1.0
        for k in range(1, SWEEPS):
            r[k] += x[k - 1]
        s = [nxt * weight * a + 2.0 * nxt / half * b for a, b in zip(s, r)]
        x = [a + b for a, b in zip(x, s)]
        weight = nxt
    return x


COEF = horner_coefficients()
LEAD = COEF[-1]


def kernel(
    tiles,
    dens_in, heat_in, laser_in, sink_in,
    sens_out, obj_out,
    dens, relay, heat, laser, sink, src, wgt, fin, *rest,
):
    near_set, far_set, rest = rest[:12], rest[12:24], rest[24:]
    (
        part, rfar, rnear, fsum, rz, nsum, nhalo, rhalo, sens, msg, arx, arz, lsem, round_sem, s_zr, r_zr, s_y, r_y, s_z, r_z, s_yf, r_yf, s_t, r_t, s_tf, r_tf, s_h, r_h, s_p, r_p, s_pz, r_pz, s_q, r_q, s_ax, r_ax, s_az, r_az,
    ) = rest
    zl_n = tiles // XC
    z_n = ZH * zl_n
    c = lax.axis_index("case")
    t = lax.axis_index("tile")
    zh = c // YD
    yy = c % YD
    zl = t // XC
    xc = t % XC
    z = zh * zl_n + zl
    has_left = t > 0
    has_right = t < tiles - 1
    halves = dens.shape[1]
    width = 128 * halves

    def y_case(d):
        return zh * YD + (yy + d) % YD

    def z_dev(d):
        zz = (z + d) % z_n
        return {"case": (zz // zl_n) * YD + yy, "tile": (zz % zl_n) * XC + xc}

    def x_tile(d):
        return zl * XC + (xc + d) % XC

    def plane_dev(k):
        return {"case": y_case(k // XC), "tile": x_tile(k % XC)}

    barrier = pltpu.get_barrier_semaphore()

    def greet(dev):
        pl.semaphore_signal(barrier, inc=1, device_id=dev, device_id_type=MESH)

    met = [z_dev(d) for d in (1, 2, 4, z_n - 1, z_n - 2, z_n - 4)]
    met += [{"case": y_case(d), "tile": t} for d in range(1, YD)]
    met += [{"case": c, "tile": x_tile(d)} for d in range(1, XC)]
    for dev in met:
        greet(dev)

    @pl.when(has_left)
    def _():
        greet({"case": c, "tile": t - 1})

    @pl.when(has_right)
    def _():
        greet({"case": c, "tile": t + 1})

    slab = pl.ds(pl.multiple_of(c * R, R), R)
    loads = []
    for h in range(halves):
        lanes = pl.ds(h * 128, 128)
        loads.append([
            pltpu.make_async_copy(dens_in.at[:, :, lanes], dens.at[pl.ds(R, R), h, slab, :], lsem.at[h, 0]),
            pltpu.make_async_copy(heat_in.at[0, :, :, lanes], heat.at[:, h], lsem.at[h, 1]),
            pltpu.make_async_copy(laser_in.at[0, :, :, lanes], laser.at[:, h], lsem.at[h, 2]),
            pltpu.make_async_copy(sink_in.at[:, :, lanes], sink.at[pl.ds(R, R), h], lsem.at[h, 3]),
        ])
    for k in range(4):
        for h in range(halves):
            loads[h][k].start()

    @pl.when(t == 0)
    def _():
        dens[0:R] = jnp.zeros((R,) + dens.shape[1:], jnp.float32)
        src[2:R] = jnp.zeros((R - 2,) + src.shape[1:], jnp.float32)
        sink[2:R] = jnp.zeros((R - 2,) + sink.shape[1:], jnp.int32)
        nhalo[0] = jnp.zeros(nhalo.shape[1:], jnp.float32)
        rhalo[0] = jnp.zeros(rhalo.shape[1:], jnp.float32)

    @pl.when(t == tiles - 1)
    def _():
        dens[2 * R:] = jnp.zeros((R,) + dens.shape[1:], jnp.float32)
        src[2 * R:3 * R - 2] = jnp.zeros((R - 2,) + src.shape[1:], jnp.float32)
        sink[2 * R:3 * R - 2] = jnp.zeros((R - 2,) + sink.shape[1:], jnp.int32)
        nhalo[1] = jnp.zeros(nhalo.shape[1:], jnp.float32)
        rhalo[1] = jnp.zeros(rhalo.shape[1:], jnp.float32)

    def make_source(l, carry):
        for j in range(R):
            for h in range(halves):
                rows = pl.ds(j * R, R)
                src[l + R, h, rows, :] = heat[l, h, rows, :] * laser[l, h, rows, :].astype(jnp.float32)
        return carry

    pl.semaphore_wait(
        barrier, len(met) + has_left.astype(jnp.int32) + has_right.astype(jnp.int32)
    )

    sends = []

    def drain():
        for guard, group in ((None, []), (has_left, []), (has_right, [])):
            group = [cp for g, cp in sends if g is guard]
            if not group:
                continue

            def wait_all(group=group):
                for cp in group:
                    cp.wait_send()

            if guard is None:
                wait_all()
            else:
                pl.when(guard)(wait_all)

    def push(cp):
        cp.start()
        sends.append((None, cp))
        return cp

    def remote(a, b, ssem, rsem, dev):
        return pltpu.make_async_remote_copy(
            src_ref=a, dst_ref=b, send_sem=ssem, recv_sem=rsem, device_id=dev, device_id_type=MESH
        )

    def to_left(a, b, ssem, rsem):
        return remote(a, b, ssem, rsem, {"case": c, "tile": jnp.maximum(t - 1, 0)})

    def to_right(a, b, ssem, rsem):
        return remote(a, b, ssem, rsem, {"case": c, "tile": jnp.minimum(t + 1, tiles - 1)})

    def piece(base, k, rows):
        return dens.at[pl.ds(base + (k // halves) * HL, HL), k % halves, rows, :]

    def piece_in(k):
        return dens_in.at[pl.ds((k // halves) * HL, HL), :, pl.ds((k % halves) * 128, 128)]

    pieces = halves * R // HL
    quarter = z_n // 4
    column = xc // 2
    via = []
    for k in range(pieces):
        way = quarter if k < pieces // 2 else z_n - quarter
        if k < pieces - 1:
            way = jnp.where(column == 0, quarter, way)
        if k > 0:
            way = jnp.where(column == XC // 2 - 1, z_n - quarter, way)
        via.append(way)
    for k in range(pieces):
        push(remote(piece_in(k), relay.at[k], s_zr.at[k], r_zr.at[k], z_dev(via[k])))
    y_copies = []
    for d in range(1, YD):
        to = {"case": y_case(d), "tile": t}
        y_copies.append([
            push(remote(piece_in(k), piece(R, k, slab), s_y.at[d - 1, k], r_y.at[d - 1, k], to))
            for k in range(pieces)
        ])

    for dev in met:
        pl.semaphore_signal(round_sem.at[0], inc=1, device_id=dev, device_id_type=MESH)
    for h in range(halves):
        loads[h][3].wait()

    halo_left = [
        to_left(src.at[pl.ds(R, R - 2)], src.at[pl.ds(2 * R, R - 2)], s_h.at[0], r_h.at[1]),
        to_left(sink.at[pl.ds(R, R - 2)], sink.at[pl.ds(2 * R, R - 2)], s_h.at[1], r_h.at[3]),
    ]
    halo_right = [
        to_right(src.at[pl.ds(R + 2, R - 2)], src.at[pl.ds(2, R - 2)], s_h.at[2], r_h.at[0]),
        to_right(sink.at[pl.ds(R + 2, R - 2)], sink.at[pl.ds(2, R - 2)], s_h.at[3], r_h.at[2]),
    ]

    def send_sides(left, right):
        @pl.when(has_left)
        def _():
            for cp in left:
                cp.start()

        @pl.when(has_right)
        def _():
            for cp in right:
                cp.start()

        sends.extend((has_left, cp) for cp in left)
        sends.extend((has_right, cp) for cp in right)

    send_sides(halo_left[1:], halo_right[1:])
    for k in range(3):
        for h in range(halves):
            loads[h][k].wait()
    lax.fori_loop(0, R, make_source, 0)
    send_sides(halo_left[:1], halo_right[:1])

    def slab_of(case):
        return pl.ds(pl.multiple_of(case * R, R), R)

    tile_copies = []

    def forward(case, order):
        rows = slab_of(case)
        here = dens.at[pl.ds(R, R), :, rows, :]
        left = to_left(here, dens.at[pl.ds(2 * R, R), :, rows, :], s_t.at[0, order], r_t.at[1, order])
        right = to_right(here, dens.at[pl.ds(0, R), :, rows, :], s_t.at[1, order], r_t.at[0, order])
        send_sides([left], [right])
        tile_copies.append((left, right))

    def forward_piece(case, order, k):
        rows = slab_of(case)
        here = piece(R, k, rows)
        left = to_left(here, piece(2 * R, k, rows), s_tf.at[0, order, k], r_tf.at[1, order, k])
        right = to_right(here, piece(0, k, rows), s_tf.at[1, order, k], r_tf.at[0, order, k])
        send_sides([left], [right])
        tile_copies.append((left, right))

    forward(c, 0)
    for d in range(1, YD):
        for cp in y_copies[d - 1]:
            cp.wait_recv()
        forward(zh * YD + (yy + YD - d) % YD, d)


    z_copies = []
    for k in range(pieces):
        into = relay.at[k]
        remote(into, into, s_zr.at[k], r_zr.at[k], z_dev(via[k])).wait_recv()
        origin = z_dev(z_n - via[k])["case"]
        z_copies.append(
            push(remote(into, piece(R, k, slab_of(origin)), s_z.at[k], r_z.at[k], z_dev(via[k])))
        )
    pl.semaphore_wait(round_sem.at[0], len(met))
    for dev in met:
        pl.semaphore_signal(round_sem.at[1], inc=1, device_id=dev, device_id_type=MESH)

    far = (1 - zh) * YD
    far_case = far + yy
    yf_copies = []

    def cross(k):
        z_copies[k].wait_recv()
        here = piece(R, k, slab_of(far_case))
        yf_copies.append({
            d: push(remote(here, here, s_yf.at[d - 1, k], r_yf.at[d - 1, k], {"case": y_case(d), "tile": t}))
            for d in (2, 1, 3)
        })
        forward_piece(far_case, 0, k)

    def spread(k):
        for d in (1, 3, 2):
            yf_copies[k][d].wait_recv()
            forward_piece(far + (yy + YD - d) % YD, d, k)

    for k in range(pieces):
        cross(k)

    def wait_sides(left, right):
        @pl.when(has_left)
        def _():
            for cp in right:
                cp.wait_recv()

        @pl.when(has_right)
        def _():
            for cp in left:
                cp.wait_recv()

    def wait_tiles(pairs):
        wait_sides([left for left, _ in pairs], [right for _, right in pairs])

    lane = lax.broadcasted_iota(jnp.int32, (R, width), 1)
    sub = lax.broadcasted_iota(jnp.int32, (R, width), 0)
    z_first = lane == 0
    z_last = lane == width - 1
    y_first = sub == 0
    y_last = sub == R - 1
    zero = jnp.zeros((R, width), jnp.float32)
    one = jnp.ones((R, width), jnp.float32)
    grid_rows = tiles * R

    def z_prev(v):
        return pltpu.roll(v, 1, 1)

    def z_next(v):
        return pltpu.roll(v, width - 1, 1)

    lane_h = lax.broadcasted_iota(jnp.int32, (R, 128), 1)

    def z_from_prev(v):
        turned = [pltpu.roll(v[:, h * 128:(h + 1) * 128], 1, 1) for h in range(halves)]
        out = turned[:1] + [jnp.where(lane_h == 0, turned[h - 1], turned[h]) for h in range(1, halves)]
        return jnp.concatenate(out, axis=1)

    def z_from_next(v):
        turned = [pltpu.roll(v[:, h * 128:(h + 1) * 128], 127, 1) for h in range(halves)]
        out = [jnp.where(lane_h == 127, turned[h + 1], turned[h]) for h in range(halves - 1)] + turned[-1:]
        return jnp.concatenate(out, axis=1)

    def flag(cond_):
        return cond_.astype(jnp.float32)

    def inside(g):
        return (g >= 0) & (g < grid_rows)

    class Rows:
        def __init__(self, base, count, refs, near=None):
            self.base, self.count, self.near = base, count, near
            self.cond, *self.ks = refs[:7]
            self.ys = refs[7:]
            self.low = 0.0 if near is None else flag(zh == 0)
            self.high = 0.0 if near is None else flag(zh == 1)

        def rows(self, j):
            return pl.ds(self.base + j, R, stride=self.count)

        def load(self, ref, e, j):
            return jnp.concatenate([ref[e, h, self.rows(j), :] for h in range(halves)], axis=1)

        def store(self, ref, e, j, value):
            for h in range(halves):
                ref[e, h, self.rows(j), :] = value[:, h * 128:(h + 1) * 128]

        def around(self, planes, outer=None):
            first = pltpu.roll(planes[-1], 1, 0)
            last = pltpu.roll(planes[0], R - 1, 0)
            if outer is not None:
                first = jnp.where(y_first, outer[0], first)
                last = jnp.where(y_last, outer[1], last)
            return [first] + planes[:-1], planes[1:] + [last]

        def outer(self, get):
            if self.near is None:
                return None
            return get(self.near, YD - 1)[5:6], get(self.near, 0)[2:3]

    def physical_step(e, part_):
        g = t * R - R + e
        nx = 2.0 + flag(g > 0) + flag(g < grid_rows - 1)
        nyz = nx + jnp.where(z_first | z_last, 1.0, 2.0)
        planes = [part_.load(dens, e, j) for j in range(part_.count)]
        outside = None
        if part_.near is not None:
            outside = [
                jnp.concatenate([dens[e, h, y:y + 1, :] for h in range(halves)], axis=1)
                for y in (3 * R - 1, 5 * R)
            ]
        befores, afters = part_.around(planes, outside)
        for j in range(part_.count):
            v, before, after = planes[j], befores[j], afters[j]
            ny = 2.0
            if j == 0:
                has = jnp.where(y_first, part_.low, 1.0)
                before = before * has
                ny = 1.0 + has
            if j == part_.count - 1:
                has = jnp.where(y_last, part_.high, 1.0)
                after = after * has
                ny = 1.0 + has
            total = (
                2.0 * v + part_.load(dens, e - 1, j) + part_.load(dens, e + 1, j) + before + after
                + jnp.where(z_first, 0.0, z_prev(v)) + jnp.where(z_last, 0.0, z_next(v))
            )
            inv = 1.0 / (nyz + ny)
            phys = total * inv
            sq = phys * phys
            part_.cond[e, j] = low_cond + (1.0 - low_cond) * (sq * phys)
            part_.store(wgt, e, j, (-1.5 * (1.0 - low_cond) * LEAD * LEAD) * sq * inv)

    def face_step(e, part_):
        g = t * R - R + e
        vm = 0.5 * flag(inside(g - 1) & inside(g))
        vp = 0.5 * flag(inside(g) & inside(g + 1))
        cond = part_.cond
        planes = [cond[e, j] for j in range(part_.count)]
        befores, afters = part_.around(planes, part_.outer(lambda near, j: near.cond[e, j]))
        for j in range(part_.count):
            v = planes[j]
            f_xm = vm * (cond[e - 1, j] + v)
            f_xp = vp * (cond[e + 1, j] + v)
            f_ym = 0.5 * (befores[j] + v)
            f_yp = 0.5 * (afters[j] + v)
            if j == 0:
                f_ym = f_ym * jnp.where(y_first, part_.low, 1.0)
            if j == part_.count - 1:
                f_yp = f_yp * jnp.where(y_last, part_.high, 1.0)
            f_zm = jnp.where(z_first, 0.0, 0.5 * (z_prev(v) + v))
            f_zp = jnp.where(z_last, 0.0, 0.5 * (z_next(v) + v))
            diag = heat_loss + f_xm + f_xp + f_ym + f_yp + f_zm + f_zp
            free = jnp.where(part_.load(sink, e, j) == 0, 1.0, 0.0)
            scale = free / diag
            for ref, face in zip(part_.ks, (f_xm, f_xp, f_ym, f_yp, f_zm, f_zp)):
                ref[e, j] = scale * face
            source = part_.load(src, e, j)
            part_.ys[0][0, e, j] = scale * source
            part_.ys[0][1, e, j] = jnp.where(source > 0.0, scale, 0.0)

    def sweep_step(n, e, part_):
        ratio = COEF[SWEEPS - 2 - n] / LEAD
        bias, y_in = part_.ys[0], part_.ys[n]
        for f in range(2):
            planes = [y_in[f, e, j] for j in range(part_.count)]
            befores, afters = part_.around(planes, part_.outer(lambda near, j: near.ys[n][f, e, j]))
            for j in range(part_.count):
                ks = [ref[e, j] for ref in part_.ks]
                acc = ratio * bias[f, e, j]
                acc = acc + ks[0] * y_in[f, e - 1, j]
                acc = acc + ks[1] * y_in[f, e + 1, j]
                acc = acc + ks[2] * befores[j]
                acc = acc + ks[3] * afters[j]
                acc = acc + ks[4] * z_from_prev(planes[j])
                acc = acc + ks[5] * z_from_next(planes[j])
                if n == SWEEPS - 2:
                    part_.store(fin.at[f], e, j, acc)
                else:
                    part_.ys[n + 1][f, e, j] = acc

    def over_layers(step, low, high, unroll=1):
        def body(e, carry):
            step(e)
            return carry

        lax.fori_loop(low, high, body, 0, unroll=unroll)

    def set_up_rows(part_, low=1, high=EXT - 1):
        over_layers(lambda e: physical_step(e, part_), low, high, 2)

    def face_rows(part_, low=2, high=EXT - 2):
        over_layers(lambda e: face_step(e, part_), low, high, 2)

    def solve_rows(part_):
        for n in range(SWEEPS - 1):
            over_layers(lambda e, n=n: sweep_step(n, e, part_), 3 + n, EXT - 3 - n, UNROLL[n])

    near = Rows(zh * (YD * R), YD, near_set)
    beyond = Rows((1 - zh) * (3 * R), YD + 1, far_set, near)
    wait_tiles(tile_copies[:YD])
    set_up_rows(near)
    wait_sides(halo_left, halo_right)
    face_rows(near)
    for k in range(pieces):
        spread(k)
    solve_rows(near)
    set_up_rows(beyond, R + 1, 2 * R - 1)
    face_rows(beyond, R + 2, 2 * R - 2)
    wait_tiles(tile_copies[YD:])
    set_up_rows(beyond, 1, R + 1)
    set_up_rows(beyond, 2 * R - 1, EXT - 1)
    face_rows(beyond, 2, R + 2)
    face_rows(beyond, 2 * R - 2, EXT - 2)
    solve_rows(beyond)

    def row_load(ref, e, k):
        return jnp.concatenate([ref[e, h, k * R:(k + 1) * R, :] for h in range(halves)], axis=1)

    def slab_store(row, value):
        for h in range(halves):
            part[h, pl.ds(row, value.shape[0]), :] = value[:, h * 128:(h + 1) * 128]

    def product_step(e, total):
        g = t * R - R + e
        l = e - R
        vm = flag(inside(g - 1))
        vp = flag(inside(g + 1))
        ps = [row_load(fin.at[0], e, k) for k in range(R)]
        qs = [row_load(fin.at[1], e, k) for k in range(R)]
        down = []
        for k in range(R):
            up = min(k + 1, R - 1)
            pn = jnp.where(y_last, pltpu.roll(ps[up], R - 1, 0), pltpu.roll(ps[k], R - 1, 0))
            qn = jnp.where(y_last, pltpu.roll(qs[up], R - 1, 0), pltpu.roll(qs[k], R - 1, 0))
            face = (ps[k] - pn) * (qs[k] - qn)
            if k == R - 1:
                face = jnp.where(y_last, 0.0, face)
            down.append((face, pltpu.roll(face, 1, 0)))
        for k in range(R):
            p, q = ps[k], qs[k]
            acc = vm * ((p - row_load(fin.at[0], e - 1, k)) * (q - row_load(fin.at[1], e - 1, k)))
            acc = acc + vp * ((p - row_load(fin.at[0], e + 1, k)) * (q - row_load(fin.at[1], e + 1, k)))
            above = down[k - 1][1] if k > 0 else 0.0
            acc = acc + down[k][0] + jnp.where(y_first, above, down[k][1])
            face = jnp.where(z_last, 0.0, (p - z_next(p)) * (q - z_next(q)))
            acc = (acc + face + z_prev(face)) * row_load(wgt, e, k)
            slab_store(pl.multiple_of(k * 10 * R + l * R, R), acc)
            if k < R - 1:
                slab_store((k + 1) * 10 * R + 8 * R + l, acc[R - 1:])
            if k > 0:
                slab_store((k - 1) * 10 * R + 9 * R + l, acc[:1])
            total = total + jnp.where(row_load(src, e, k) > 0.0, p, 0.0)
        return total

    for h in range(halves):
        part[h, 8 * R:9 * R, :] = jnp.zeros((R, 128), jnp.float32)
        part[h, 7 * 10 * R + 9 * R:7 * 10 * R + 10 * R, :] = jnp.zeros((R, 128), jnp.float32)

    obj_vec = lax.fori_loop(R, R + RL, product_step, zero)

    def part_rows(case, a):
        return pl.ds(pl.multiple_of(case * (10 * R) + a * RL * R, R), RL * R)

    def y_parts(side, dest_base, a, buf):
        rows = pl.ds(a * RL * R, RL * R)
        return [
            [
                push(remote(
                    part.at[h, part_rows(dest_base + (yy + d) % YD, a)], buf.at[d - 1, h, rows],
                    s_p.at[side, d - 1, h, a], r_p.at[side, d - 1, h, a], {"case": y_case(d), "tile": t},
                ))
                for d in range(1, YD)
            ]
            for h in range(halves)
        ]

    def add_parts(h, case, a, buf, out):
        base = case * (10 * R)

        def step(i, carry):
            rows = pl.ds(pl.multiple_of(i * R, R), R)
            mine = part[h, pl.ds(pl.multiple_of(base + i * R, R), R), :]
            out[h, rows, :] = (mine + buf[0, h, rows, :]) + (buf[1, h, rows, :] + buf[2, h, rows, :])
            return carry

        lax.fori_loop(a * RL, (a + 1) * RL, step, 0, unroll=RL)

    far_parts = [y_parts(0, far, 0, rfar)]
    obj_vec = lax.fori_loop(R + RL, 2 * R, product_step, obj_vec)
    far_parts.append(y_parts(0, far, 1, rfar))
    near_parts = [y_parts(1, zh * YD, a, rnear) for a in range(2)]
    obj_part = LEAD * jnp.sum(obj_vec, axis=(0, 1), keepdims=True)

    low = pl.ds(0, R)
    high = pl.ds((R - 1) * R, R)
    left_case = {"case": far_case, "tile": jnp.maximum(t - 1, 0)}
    right_case = {"case": far_case, "tile": jnp.minimum(t + 1, tiles - 1)}
    far_left = remote(fsum.at[:, low], rhalo.at[1], s_q.at[0], r_q.at[1], left_case)
    far_right = remote(fsum.at[:, high], rhalo.at[0], s_q.at[1], r_q.at[0], right_case)
    near_left = to_left(nsum.at[:, low], nhalo.at[1], s_q.at[2], r_q.at[3])
    near_right = to_right(nsum.at[:, high], nhalo.at[0], s_q.at[3], r_q.at[2])
    crossing = []
    for a in range(2):
        rows = pl.ds(a * RL * R, RL * R)
        for h in range(halves):
            for cp in far_parts[a][h]:
                cp.wait_recv()
            add_parts(h, far_case, a, rfar, fsum)
            crossing.append(push(remote(
                fsum.at[h, rows], rz.at[h, rows], s_pz.at[h, a], r_pz.at[h, a], z_dev(zl_n)
            )))
        send_sides([far_left] if a == 0 else [], [] if a == 0 else [far_right])
    for a in range(2):
        for h in range(halves):
            for cp in near_parts[a][h]:
                cp.wait_recv()
            add_parts(h, c, a, rnear, nsum)
    send_sides([near_left], [near_right])
    for cp in crossing:
        cp.wait_recv()

    @pl.when(has_left)
    def _():
        near_right.wait_recv()
        far_right.wait_recv()

    @pl.when(has_right)
    def _():
        near_left.wait_recv()
        far_left.wait_recv()

    def wide(first, second, rows):
        return jnp.concatenate([first[h, rows, :] + second[h, rows, :] for h in range(halves)], axis=1)

    every = slice(0, R)
    qs = [wide(nhalo.at[0], rhalo.at[0], every)]
    qs += [wide(nsum, rz, slice(l * R, (l + 1) * R)) for l in range(R)]
    qs += [wide(nhalo.at[1], rhalo.at[1], every)]
    abs_vec = zero
    for l in range(R):
        v = qs[l + 1]
        before = jnp.where(y_first, wide(nsum, rz, slice(8 * R + l, 8 * R + l + 1)), pltpu.roll(v, 1, 0))
        after = jnp.where(y_last, wide(nsum, rz, slice(9 * R + l, 9 * R + l + 1)), pltpu.roll(v, R - 1, 0))
        value = (
            2.0 * v + qs[l] + qs[l + 2] + before + after
            + jnp.where(z_first, 0.0, z_prev(v)) + jnp.where(z_last, 0.0, z_next(v))
        )
        sens[l] = value
        abs_vec = abs_vec + jnp.abs(value)

    pl.semaphore_wait(round_sem.at[1], len(met))
    lane1 = lax.broadcasted_iota(jnp.int32, (1, 128), 1)
    now = jnp.where(lane1 == 8, jnp.sum(abs_vec, axis=(0, 1), keepdims=True), jnp.where(lane1 == c, obj_part, 0.0))
    def ring(d, n):
        return min(d, n - d)

    plane_order = sorted(range(1, YD * XC), key=lambda k: -ring(k // XC, YD) - ring(k % XC, XC) / 2)
    z_order = sorted(range(1, z_n), key=lambda k: -ring(k, z_n))
    for i, (buf, ssem, rsem, order, dev) in enumerate(
        [(arx, s_ax, r_ax, plane_order, plane_dev), (arz, s_az, r_az, z_order, z_dev)]
    ):
        msg[i] = now
        before = list(sends)
        copies = [
            push(remote(msg.at[i], buf.at[k - 1], ssem.at[k - 1], rsem.at[k - 1], dev(k))) for k in order
        ]
        if i == 1:
            sends[:] = before
            drain()
            sends[:] = [(None, cp) for cp in copies]
        for cp in copies:
            cp.wait_recv()
        now = now + jnp.sum(buf[...], axis=0)

    total_abs = jnp.sum(jnp.where(lane1 == 8, now, 0.0), axis=(0, 1), keepdims=True)
    scale = 1.0 / (total_abs / (grid_rows * R * R * width) + 1e-06)
    obj_out[...] = jnp.zeros_like(obj_out) + jnp.sum(jnp.where(lane1 == c, now, 0.0), axis=(0, 1), keepdims=True)
    for l in range(R):
        sens_out[l] = sens[l] * scale

    drain()


def body(density, heat_power, laser_mask, sink_mask):
    tiles = lax.axis_size("tile")
    rows, grid_y, width = sink_mask.shape
    halves = width // 128
    pieces = halves * R // HL
    f32 = jnp.float32
    z_n = ZH * (tiles // XC)

    def vm(*shape):
        return pltpu.VMEM(shape, f32)

    def dma(*shape):
        return pltpu.SemaphoreType.DMA(shape)

    scratch = [
        vm(EXT, halves, grid_y, 128),
        vm(pieces, HL, R, 128),
        vm(rows, halves, grid_y, 128),
        pltpu.VMEM((rows, halves, grid_y, 128), jnp.int32),
        pltpu.VMEM((EXT, halves, grid_y, 128), jnp.int32),
        vm(EXT, halves, grid_y, 128),
        vm(EXT, halves, grid_y, 128),
        vm(2, EXT, halves, grid_y, 128),
    ]
    for count in (YD, YD + 1):
        scratch += [vm(EXT, count, R, width)] * 7 + [vm(2, EXT, count, R, width)] * (SWEEPS - 1)
    scratch += [
        vm(halves, 8 * 10 * R, 128),
        vm(YD - 1, halves, 10 * R, 128),
        vm(YD - 1, halves, 10 * R, 128),
        vm(halves, 10 * R, 128),
        vm(halves, 10 * R, 128),
        vm(halves, 10 * R, 128),
        vm(2, halves, R, 128),
        vm(2, halves, R, 128),
        vm(R, R, width),
        vm(2, 1, 128),
        vm(YD * XC - 1, 1, 128),
        vm(z_n - 1, 1, 128),
        dma(halves, 4),
        pltpu.SemaphoreType.REGULAR((2,)),
        dma(pieces), dma(pieces),
        dma(YD - 1, pieces), dma(YD - 1, pieces),
        dma(pieces), dma(pieces),
        dma(YD - 1, pieces), dma(YD - 1, pieces),
        dma(2, YD), dma(2, YD),
        dma(2, YD, pieces), dma(2, YD, pieces),
        dma(4), dma(4),
        dma(2, YD - 1, halves, 2), dma(2, YD - 1, halves, 2),
        dma(halves, 2), dma(halves, 2),
        dma(4), dma(4),
        dma(YD * XC - 1), dma(YD * XC - 1),
        dma(z_n - 1), dma(z_n - 1),
    ]
    any_spec = pl.BlockSpec(memory_space=pl.ANY)
    vmem_spec = pl.BlockSpec(memory_space=pltpu.VMEM)
    sensitivity, objective = pl.pallas_call(
        functools.partial(kernel, tiles),
        out_shape=(
            jax.ShapeDtypeStruct(density.shape, f32),
            jax.ShapeDtypeStruct((1, 128), f32),
        ),
        in_specs=[any_spec] * 4,
        out_specs=(vmem_spec, vmem_spec),
        scratch_shapes=scratch,
        compiler_params=pltpu.CompilerParams(
            collective_id=0, has_side_effects=True, vmem_limit_bytes=56460000
        ),
    )(density, heat_power, laser_mask, sink_mask)
    return sensitivity, objective[0, :1]


def solution(mesh):
    return jax.shard_map(
        body,
        mesh=mesh,
        in_specs=(
            P("tile", "case", None),
            P("case", "tile", None, None),
            P("case", "tile", None, None),
            P("tile", None, None),
        ),
        out_specs=(P("tile", "case", None), P("case")),
        check_vma=False,
    )
```
